32 devices in a mesh: gx: 8 (over z, core), gy: 4 (over y, x).
Axes of the slice: x: 2, y: 2, z: 4, core: 2. Of those that a mesh axis runs over, the one named last changes fastest.
Arguments:
- rhs: float32 [64, 32, 6, 3, 256], P('gx', 'gy'), may hold values from -400 to 400
- contrast: float32 [64, 32, 256], P('gx', 'gy'), may hold values from 0.2 to 2
- occupied: int32 [64, 32], P('gx', 'gy'), may hold values 0 or 1
- near: bfloat16 [5, 768, 768], replicated, may hold values from -0.078125 to 0.078125
- basis: bfloat16 [768, 64], replicated, may hold values from -0.21875 to 0.21875
- transfer: float32 [4, 4, 64, 64], replicated, may hold values from -0.5 to 0.5
- coupling: float32 [5, 20, 64, 64], replicated, may hold values from -0.15625 to 0.15625
Outputs:
- third: float32 [64, 32, 6, 3, 256], P('gx', 'gy')
- hess: float32 [6, 6], replicated
The draws below stay inside these ranges and needn't reach their ends.
All inputs are finite; a program needn't handle non-finite values. No bound on the sum of `occupied` on one device may be relied on, other than what follows from the above.
Results may differ from the reference program's by a relative error of at most 0.0031.
Values may be sent and summed in bfloat16 or wider, within the bound.
A program may use at most 128 MiB of HBM per device.

```python
import math
import jax
import jax.numpy as jnp
from jax import lax

P_SIZE = 256
R = 64
NRHS = 6
NLX = 64
NLY = 32
LEVELS = 5


def draw_rhs(key, part):
    key_base = jax.random.fold_in(key, 11)
    key_values, key_box, key_voxel = jax.random.split(key_base, 3)
    shape_all = (NLX, NLY, NRHS, 3, P_SIZE)
    values_drawn = jnp.clip(jax.random.normal(key_values, shape_all, jnp.float32), -4.0, 4.0)
    box_scale = jnp.exp(math.log(10.0) * jax.random.uniform(key_box, (NLX, NLY), jnp.float32))
    rising = 1.0 + 2.0 * jnp.arange(NLX, dtype=jnp.float32) / NLX
    voxel_scale = jnp.exp(math.log(3.0) * jax.random.uniform(key_voxel, (P_SIZE,), jnp.float32))
    return values_drawn * (box_scale * rising[:, None])[:, :, None, None, None] * voxel_scale


def touch_ends(drawn, own_key, low, largest):
    spot = [jax.random.randint(jax.random.fold_in(own_key, axis), (), 0, length) for axis, length in enumerate(drawn.shape)]
    widest = drawn.shape.index(max(drawn.shape))
    next_to = spot[:widest] + [(spot[widest] + 1) % drawn.shape[widest]] + spot[widest + 1:]
    return drawn.at[tuple(spot)].set(low).at[tuple(next_to)].set(largest)


def levels(rng, dims, pieces, least, largest):
    loudness, own = 1.0, jax.random.fold_in(rng, 6)
    for axis_at, blocks in pieces:
        steps = jnp.exp(jax.random.uniform(jax.random.fold_in(own, axis_at), (blocks,), jnp.float32, least / len(pieces), largest / len(pieces)))
        loudness = loudness * jnp.repeat(steps, dims[axis_at] // blocks).reshape([-1 if axis == axis_at else 1 for axis in range(len(dims))])
    return loudness


def gaussian(stream_key, extent, scale, bound, kind=jnp.bfloat16):
    return jnp.clip(scale * jax.random.normal(stream_key, extent, jnp.float32), -bound, bound).astype(kind)


def setup_inputs(seed: int = 0) -> dict:
    keys = jax.random.split(jax.random.key(seed), 8)
    return {
        "rhs": draw_rhs(jax.random.fold_in(keys[7], 71), 0),
        "contrast": jnp.clip(jnp.exp(math.log(2.0) - 2.3025851 * jax.random.uniform(keys[1], (NLX, NLY, P_SIZE), jnp.float32) ** levels(keys[1], (NLX, NLY, P_SIZE), ((0, 8), (1, 4)), -0.2, 0.2)), 0.2, 2.0),
        "occupied": touch_ends((jax.random.randint(keys[2], (NLX, NLY), 0, 4) < 3).astype(jnp.int32), jax.random.fold_in(keys[2], 1), 0, 1),
        "near": gaussian(keys[3], (5, 3 * P_SIZE, 3 * P_SIZE), (27 * P_SIZE) ** -0.5, 0.078125),
        "basis": gaussian(keys[4], (3 * P_SIZE, R), (3 * P_SIZE) ** -0.5, 0.21875),
        "transfer": gaussian(keys[5], (LEVELS - 1, 4, R, R), (2 * R) ** -0.5, 0.5, jnp.float32),
        "coupling": gaussian(keys[6], (LEVELS, 20, R, R), (27 * R) ** -0.5, 0.15625, jnp.float32),
    }


PRECISE = lax.Precision.HIGHEST
EPSILON = 1e-06
NEAR_BASE = ((0, 0), (1, -1), (1, 0), (1, 1), (0, 1))

def near_terms():
    listing = []
    for slot_index, (shift_x, shift_y) in enumerate(NEAR_BASE):
        listing.append((shift_x, shift_y, slot_index, False))
        if shift_x != 0 or shift_y != 0:
            listing.append((-shift_x, -shift_y, slot_index, True))
    return listing

def far_terms():
    base_list = []
    for shift_x in range(-3, 4):
        for shift_y in range(-3, 4):
            if max(abs(shift_x), abs(shift_y)) >= 2 and (shift_x > 0 or (shift_x == 0 and shift_y > 0)):
                base_list.append((shift_x, shift_y))
    listing = []
    for slot_index, (shift_x, shift_y) in enumerate(base_list):
        listing.append((shift_x, shift_y, slot_index, False))
        listing.append((-shift_x, -shift_y, slot_index, True))
    return listing

def parent_close(parity, offset):
    return jnp.abs((parity + offset) // 2) <= 1

def lift(skeleton, matrices):
    size_x, size_y, fields, rank = skeleton.shape
    fold_x = 2 if size_x > 1 else 1
    fold_y = 2 if size_y > 1 else 1
    blocks = skeleton.reshape(size_x // fold_x, fold_x, size_y // fold_y, fold_y, fields, rank)
    total = jnp.zeros((size_x // fold_x, size_y // fold_y, fields, rank), jnp.float32)
    for child_x in range(fold_x):
        for child_y in range(fold_y):
            piece = blocks[:, child_x, :, child_y].reshape(-1, rank)
            total = total + jnp.dot(piece, matrices[2 * child_x + child_y], precision=PRECISE).reshape(total.shape)
    return total

def lower(parent, matrices, size_x, size_y):
    par_x, par_y, fields, rank = parent.shape
    fold_x = size_x // par_x
    fold_y = size_y // par_y
    flat_parent = parent.reshape(-1, rank)
    rows_list = []
    for child_x in range(fold_x):
        cols_list = []
        for child_y in range(fold_y):
            cols_list.append(jnp.dot(flat_parent, matrices[2 * child_x + child_y].T, precision=PRECISE).reshape(parent.shape))
        rows_list.append(jnp.stack(cols_list, axis=2))
    return jnp.stack(rows_list, axis=1).reshape(size_x, size_y, fields, rank)

def couple_padded(padded, size_x, size_y, matrices):
    fields, rank = (padded.shape[2], padded.shape[3])
    parity_x = jnp.arange(size_x, dtype=jnp.int32) % 2
    parity_y = jnp.arange(size_y, dtype=jnp.int32) % 2
    total = jnp.zeros((size_x, size_y, fields, rank), jnp.float32)
    for shift_x, shift_y, slot_index, flipped in far_terms():
        block = matrices[slot_index].T if flipped else matrices[slot_index]
        piece = padded[3 + shift_x:3 + shift_x + size_x, 3 + shift_y:3 + shift_y + size_y].reshape(-1, rank)
        keep = (parent_close(parity_x, shift_x)[:, None] & parent_close(parity_y, shift_y)[None, :]).astype(jnp.float32)
        total = total + keep[:, :, None, None] * jnp.dot(piece, block, precision=PRECISE).reshape(size_x, size_y, fields, rank)
    return total

def couple(skeleton, matrices):
    padded = jnp.pad(skeleton, ((3, 3), (3, 3), (0, 0), (0, 0)))
    return couple_padded(padded, skeleton.shape[0], skeleton.shape[1], matrices)

def apply_operator(field, occupied, contrast, near, basis, transfer, coupling):
    source = (occupied.astype(jnp.float32)[:, :, None, None, None] * contrast[:, :, None, None, :] * field).astype(jnp.bfloat16)
    size_x, size_y, fields = (source.shape[0], source.shape[1], source.shape[2])
    width = source.shape[3] * source.shape[4]
    rank = basis.shape[1]
    flat_source = source.reshape(size_x, size_y, fields, width)
    padded = jnp.pad(flat_source, ((1, 1), (1, 1), (0, 0), (0, 0)))
    near_sum = jnp.zeros((size_x, size_y, fields, width), jnp.float32)
    for shift_x, shift_y, slot_index, flipped in near_terms():
        block = near[slot_index].T if flipped else near[slot_index]
        piece = padded[1 + shift_x:1 + shift_x + size_x, 1 + shift_y:1 + shift_y + size_y].reshape(-1, width)
        near_sum = near_sum + jnp.dot(piece, block, preferred_element_type=jnp.float32).reshape(size_x, size_y, fields, width)
    skeleton = [jnp.dot(flat_source.reshape(-1, width), basis, preferred_element_type=jnp.float32).reshape(size_x, size_y, fields, rank)]
    for depth in range(LEVELS - 1):
        skeleton.append(lift(skeleton[-1], transfer[depth]))
    down = couple(skeleton[LEVELS - 1], coupling[LEVELS - 1])
    for depth in range(LEVELS - 2, -1, -1):
        child = skeleton[depth]
        down = couple(child, coupling[depth]) + lower(down, transfer[depth], child.shape[0], child.shape[1])
    far_part = jnp.dot(down.reshape(-1, rank), basis.T.astype(jnp.float32), precision=PRECISE).reshape(size_x, size_y, fields, width)
    return field + (near_sum + far_part).reshape(field.shape)

def reference(rhs, contrast, occupied, near, basis, transfer, coupling):

    def inner(first_arr, second_arr):
        return lax.optimization_barrier(jnp.mean(first_arr * second_arr, axis=(0, 1, 3, 4)))

    def spread(values):
        return values[None, None, :, None, None]

    def operate(field):
        return apply_operator(field, occupied, contrast, near, basis, transfer, coupling)
    scale_start = jnp.sqrt(inner(rhs, rhs) + EPSILON)
    first = rhs / spread(scale_start)
    image = operate(first)
    coef_first = inner(first, image)
    rest = image - spread(coef_first) * first
    norm_first = jnp.sqrt(inner(rest, rest) + EPSILON)
    second = rest / spread(norm_first)
    image = operate(second)
    coef_cross = inner(first, image)
    coef_second = inner(second, image)
    rest = image - spread(coef_cross) * first - spread(coef_second) * second
    norm_second = jnp.sqrt(inner(rest, rest) + EPSILON)
    third = rest / spread(norm_second)
    hess = jnp.stack([scale_start, coef_first, norm_first, coef_cross, coef_second, norm_second], axis=1)
    return (third, hess)
```

```python
import functools

import jax
import jax.numpy as jnp
from jax import lax
from jax.experimental import pallas as pl
from jax.experimental.pallas import tpu as pltpu
from jax.sharding import PartitionSpec as P

EPSILON = 1e-06
SHRINK = 2.0**-20
NEAR_BASE = ((0, 0), (1, -1), (1, 0), (1, 1), (0, 1))
HALF_RING = NEAR_BASE[1:]
AROUND = [(a, b) for a in (-1, 0, 1) for b in (-1, 0, 1)]
COMPASS = [d for d in AROUND if d != (0, 0)]
CHILDREN = [(c, e) for c in (0, 1) for e in (0, 1)]
MESH = pl.DeviceIdType.MESH
F32 = jnp.float32
BF16 = jnp.bfloat16


def near_lookup():
    table = {}
    for slot, (a, b) in enumerate(NEAR_BASE):
        table[(a, b)] = (slot, False)
        if (a, b) != (0, 0):
            table[(-a, -b)] = (slot, True)
    return table


def far_lookup():
    base = [
        (a, b)
        for a in range(-3, 4)
        for b in range(-3, 4)
        if max(abs(a), abs(b)) >= 2 and (a > 0 or (a == 0 and b > 0))
    ]
    table = {}
    for slot, (a, b) in enumerate(base):
        table[(a, b)] = (slot, False)
        table[(-a, -b)] = (slot, True)
    return table


def halves(values):
    high = values.astype(BF16)
    return high, (values - high.astype(F32)).astype(BF16)


def far_level(depth, coupling, far):
    table = far_lookup()
    rank = coupling.shape[2]
    empty = jnp.zeros((rank, rank), F32)
    seen = {}

    def block_of(offset):
        if offset not in table:
            return empty
        if offset not in seen:
            slot, flipped = table[offset]
            block = coupling[depth, slot]
            seen[offset] = block.T if flipped else block
        return seen[offset]

    for i, (px, py) in enumerate(HALF_RING):
        for k, (c, e) in enumerate(CHILDREN):
            line = [block_of((2 * px + c - tc, 2 * py + e - te)) for tc, te in CHILDREN]
            high, low = halves(jnp.concatenate(line, axis=1))
            far[depth, i, 0, k * rank : (k + 1) * rank, :] = high
            far[depth, i, 1, k * rank : (k + 1) * rank, :] = low


def strip(move, length):
    if move > 0:
        return pl.ds(length, 1), pl.ds(0, 1)
    if move < 0:
        return pl.ds(1, 1), pl.ds(length + 1, 1)
    return pl.ds(1, length), pl.ds(1, length)


def stacked(values):
    high = values.astype(BF16).astype(F32)
    return jnp.concatenate([high, values - high], axis=0).astype(BF16)


def product(left, right, across=1):
    return lax.dot_general(
        left, right, (((1,), (1 - across,)), ((), ())), preferred_element_type=F32
    )


def times(values, high, low, across=1):
    both = stacked(values)
    total = product(both, high, across) + product(both, low, across)
    rows = values.shape[0]
    return total[:rows] + total[rows:]


def group(boxes, size_x, size_y):
    rows = []
    for x in range(0, size_x, 2):
        for y in range(0, size_y, 2):
            four = [(x + c) * size_y + y + e for c, e in CHILDREN]
            rows.append(jnp.concatenate([boxes[8 * i : 8 * i + 8] for i in four], axis=1))
    return rows


def child_of(parents, x, y, size_y):
    rank = parents.shape[1] // 4
    i = (x // 2) * size_y + y // 2
    k = 2 * (x % 2) + y % 2
    return parents[8 * i : 8 * i + 8, k * rank : (k + 1) * rank]


def ungroup(parents, size_x, size_y):
    return jnp.concatenate(
        [child_of(parents, x, y, size_y) for x in range(2 * size_x) for y in range(2 * size_y)],
        axis=0,
    )


def clear_rim(out):
    long_x, long_y = out.shape[0], out.shape[1]
    line_x = jnp.zeros((1,) + out.shape[1:], out.dtype)
    line_y = jnp.zeros((long_x, 1) + out.shape[2:], out.dtype)
    out[0:1] = line_x
    out[long_x - 1 : long_x] = line_x
    out[:, 0:1] = line_y
    out[:, long_y - 1 : long_y] = line_y


def fold(value):
    pieces = [value[:, i : i + 128] for i in range(0, value.shape[1], 128)]
    return functools.reduce(lambda a, b: a + b, pieces)


def krylov_kernel(size_x, size_y, inner, count, *refs):
    arguments, (third, hess), scratch = refs[:7], refs[7:9], refs[9:]
    rhs, contrast, occupied, near, basis, lifts, coupling = scratch[:7]
    far, lift_high, lift_low, basis_twice, weight, product_of, source = scratch[7:14]
    image, total, skeleton, edge_send, edge, corner, edge_wide, corner_wide = scratch[14:22]
    bands = scratch[22 : 22 + inner]
    rest = scratch[22 + inner :]
    levels = coupling.shape[0]
    coarse = levels - inner
    tops = rest[:coarse]
    mine, gathered, parts, slots = rest[coarse : coarse + 4]
    near_send, near_receive, band_send, band_receive = rest[coarse + 4 : coarse + 8]
    gather_send, gather_receive, sum_send, sum_receive, load, unload = rest[coarse + 8 :]

    side, fields, comps, _, voxels = rhs.shape
    rank, width = basis.shape
    slab = fields * side
    rows = side * slab
    devices = size_x * size_y
    me_x, me_y = lax.axis_index("gx"), lax.axis_index("gy")
    me = me_x * size_y + me_y
    chunk = 256 if width % 256 == 0 else 128
    lane = lax.broadcasted_iota(jnp.int32, (8, 128), 1)
    sublane = lax.broadcasted_iota(jnp.int32, (8, 128), 0)

    loads = [
        pltpu.make_async_copy(argument, here, load.at[i])
        for i, (argument, here) in enumerate(zip(arguments, scratch[:7]))
    ]
    for i in (0, 1, 2, 4, 5, 6, 3):
        loads[i].start()

    def wrap(value, size):
        return jnp.where(value >= size, value - size, value)

    def others(act):
        def line(shift_x):
            to_x, from_x = wrap(me_x + shift_x, size_x), wrap(me_x + size_x - shift_x, size_x)
            for shift_y in range(size_y):
                if not isinstance(shift_x, int) or (shift_x, shift_y) != (0, 0):
                    to_y = wrap(me_y + shift_y, size_y)
                    from_y = wrap(me_y + size_y - shift_y, size_y)
                    act(shift_x * size_y + shift_y, (to_x, to_y), from_x * size_y + from_y)

        if devices <= 64:
            for shift_x in range(size_x):
                line(shift_x)
        else:
            line(0)

            def one(shift_x, carry):
                line(shift_x)
                return carry

            lax.fori_loop(1, size_x, one, 0)

    for step in (0, 1):
        for side_rows in (slice(0, slab), slice((side + 1) * slab, (side + 2) * slab)):
            source[step, 1, side_rows] = jnp.zeros((slab, width), BF16)
        edge[step] = jnp.zeros(edge.shape[1:], BF16)
        corner[step] = jnp.zeros(corner.shape[1:], BF16)
        for band in bands:
            clear_rim(band.at[step])
    for top in tops:
        clear_rim(top)

    barrier = pltpu.get_barrier_semaphore()

    def greet(step, to, before):
        pl.semaphore_signal(
            barrier, inc=1, device_id={"gx": to[0], "gy": to[1]}, device_id_type=MESH
        )

    others(greet)

    def gather_copy(piece, target, sent, received, step, to, slot):
        return pltpu.make_async_remote_copy(
            src_ref=piece,
            dst_ref=target.at[slot],
            send_sem=sent.at[step],
            recv_sem=received.at[step],
            device_id={"gx": to[0], "gy": to[1]},
            device_id_type=MESH,
        )

    def start_gather(*what):
        others(lambda step, to, before: gather_copy(*what, step, to, me).start())

    def finish_gather(*what):
        others(lambda step, to, before: gather_copy(*what, step, to, before).wait())

    def sums_of(number):
        return parts.at[number], slots.at[number], sum_send.at[number], sum_receive.at[number]

    def put_sums(number, sums):
        tile = jnp.zeros((8, 128), F32)
        for i, of_fields in enumerate(sums):
            lines = [jnp.sum(value, axis=0, keepdims=True) for value in of_fields]
            lines.append(jnp.zeros((8 - fields, 128), F32))
            column = jnp.sum(jnp.concatenate(lines, axis=0), axis=1, keepdims=True)
            tile = tile + jnp.where(lane == 8 * i + sublane, column, 0.0)
        line = jnp.sum(tile, axis=0, keepdims=True)
        parts[number] = line
        slots[number, me] = line

    def finish_sums(number, amount):
        finish_gather(*sums_of(number))
        line = jnp.broadcast_to(jnp.sum(slots[number], axis=0) * (1.0 / count), (8, 128))
        return [
            jnp.sum(jnp.where(lane == 8 * i + sublane, line, 0.0), axis=1, keepdims=True)
            for i in range(amount)
        ]

    def spread(column):
        return [
            jnp.broadcast_to(column[field : field + 1, :], (8, voxels)) for field in range(fields)
        ]

    def sweep(amount, work):
        zero = tuple(jnp.zeros((8, 128), F32) for _ in range(amount * fields))

        def one(x, sums):
            sums = [list(sums[i * fields : (i + 1) * fields]) for i in range(amount)]

            def add(i, field, value):
                sums[i][field] = sums[i][field] + fold(value)

            work(x, add)
            return tuple(value for of_fields in sums for value in of_fields)

        out = lax.fori_loop(0, side, one, zero)
        return [out[i * fields : (i + 1) * fields] for i in range(amount)]

    def tiles(x):
        for field in range(fields):
            place = pl.ds(pl.multiple_of(x * slab + field * side, 8), side)
            for part in range(comps):
                yield field, part, place, slice(part * voxels, (part + 1) * voxels)

    def put_product(part, place, value):
        for i in range(voxels // 128):
            product_of[part * (voxels // 128) + i, place] = value[:, i * 128 : (i + 1) * 128]

    def put_source(step, x, values):
        for field in range(0, fields, 2):
            place = pl.ds(pl.multiple_of((x + 1) * slab + field * side, 16), 2 * side)
            for part in range(comps):
                pair = [values[field + i, part] for i in (0, 1)]
                columns = slice(part * voxels, (part + 1) * voxels)
                source[step, 1, place, columns] = jnp.concatenate(pair, axis=0).astype(BF16)

    def inside(place_x, place_y):
        return (place_x >= 0) & (place_x < size_x) & (place_y >= 0) & (place_y < size_y)

    def near_copy(step, way):
        move_x, move_y = COMPASS[way]
        if move_y == 0:
            begin, end = (side, 0) if move_x > 0 else (1, side + 1)
            from_ref = source.at[step, 1, pl.ds(begin * slab, slab)]
            to_ref = source.at[step, 1, pl.ds(end * slab, slab)]
        else:
            from_ref = edge_send.at[step, int(move_y > 0)]
            to_ref = edge.at[step, int(move_y > 0)]
            if move_x != 0:
                begin = from_ref.shape[0] - 16 if move_x > 0 else 0
                from_ref, to_ref = from_ref.at[pl.ds(begin, 16)], corner.at[step, way]
        return pltpu.make_async_remote_copy(
            src_ref=from_ref,
            dst_ref=to_ref,
            send_sem=near_send.at[step, way],
            recv_sem=near_receive.at[step, way],
            device_id={"gx": me_x + move_x, "gy": me_y + move_y},
            device_id_type=MESH,
        )

    def band_copy(number, step, way):
        move_x, move_y = COMPASS[way]
        band = bands[number].at[step]
        from_x, to_x = strip(move_x, band.shape[0] - 2)
        from_y, to_y = strip(move_y, band.shape[1] - 2)
        return pltpu.make_async_remote_copy(
            src_ref=band.at[from_x, from_y],
            dst_ref=band.at[to_x, to_y],
            send_sem=band_send.at[number, step, way],
            recv_sem=band_receive.at[number, step, way],
            device_id={"gx": me_x + move_x, "gy": me_y + move_y},
            device_id_type=MESH,
        )

    def near_copies(step):
        return [functools.partial(near_copy, step)]

    def band_copies(step):
        return [functools.partial(band_copy, number, step) for number in range(inner)]

    def start_copies(copies):
        for way, (move_x, move_y) in enumerate(COMPASS):

            @pl.when(inside(me_x + move_x, me_y + move_y))
            def _(way=way):
                for copy in copies:
                    copy(way).start()

    def finish_copies(copies):
        for way, (move_x, move_y) in enumerate(COMPASS):

            @pl.when(inside(me_x + move_x, me_y + move_y))
            def _(way=way):
                for copy in copies:
                    copy(way).wait_send()

            @pl.when(inside(me_x - move_x, me_y - move_y))
            def _(way=way):
                for copy in copies:
                    copy(way).wait_recv()

    def cut_edges(step):
        for i, y in enumerate((0, side - 1)):
            for part in range(width // 128):
                line = product_of[part, pl.ds(y, side * fields, stride=side), :]
                edge_send[step, i, :, part * 128 : (part + 1) * 128] = line.astype(BF16)

    def upward(step):
        own = source[step, 1, slab : slab + rows]
        skeleton[0:rows, 0:rank] = product(own, basis[...], 0)
        parents = []
        for x in range(0, side, 2):
            for y in range(0, side, 2):
                four = [
                    skeleton[pl.ds((x + c) * slab + y + e, 8, stride=side), :][:, :rank]
                    for c, e in CHILDREN
                ]
                parents.append(jnp.concatenate(four, axis=1))
        span = side
        for depth in range(inner):
            span //= 2
            for i, parent in enumerate(parents):
                bands[depth][step, 1 + i // span, 1 + i % span] = parent
            level = times(jnp.concatenate(parents, axis=0), lift_high[depth], lift_low[depth])
            if depth < inner - 1:
                parents = group(level, span, span)
        mine[step] = level
        gathered[step, me] = level

    def gather_of(step):
        return mine.at[step], gathered.at[step], gather_send.at[step], gather_receive.at[step]

    table = near_lookup()

    def near_term(step, a, b, columns):
        slot, flipped = table[(a, b)]
        piece = source[step, 1 + b, (1 + a) * slab : (1 + a) * slab + rows]
        if flipped:
            return product(piece, near[slot, columns, :], 0)
        return product(piece, near[slot, :, columns])

    def widen_edges(step):
        for i in (0, 1):
            edge_wide[i] = edge[step, i].astype(F32)
        for way, (move_x, move_y) in enumerate(COMPASS):
            if move_x != 0 and move_y != 0:
                corner_wide[way] = corner[step, way].astype(F32)

    pieces = chunk // 128
    row_of = lax.broadcasted_iota(jnp.int32, (side, chunk), 0)

    def shift_columns(step, b, index, columns):
        last = side - 1 if b > 0 else 0
        for x in range(-1, side + 1):
            shifted = []
            if x in (-1, side):
                place = slice((x + 1) * slab, (x + 2) * slab)
                own = source[step, 1, place, columns].astype(F32)
                way = COMPASS.index((1 if x < 0 else -1, -b))
                begin = 16 - fields if x < 0 else 0
            else:
                lines = slice(x * slab, (x + 1) * slab)
                own = [product_of[index * pieces + i, lines] for i in range(pieces)]
                own = jnp.concatenate(own, axis=1)
            for field in range(fields):
                value = pltpu.roll(
                    own[field * side : (field + 1) * side], side - 1 if b > 0 else 1, 0
                )
                if x in (-1, side):
                    beyond = corner_wide[way, begin + field : begin + field + 1, columns]
                else:
                    i = x * fields + field
                    beyond = edge_wide[int(b < 0), i : i + 1, columns]
                beyond = jnp.broadcast_to(beyond, value.shape)
                shifted.append(jnp.where(row_of == last, beyond, value))
            for field in range(0, fields, 2):
                begin_row = (x + 1) * slab + field * side
                source[step, 1 + b, begin_row : begin_row + 2 * side, columns] = jnp.concatenate(
                    shifted[field : field + 2], axis=0
                ).astype(BF16)

    def over_columns(work):
        def one(index, carry):
            work(index, pl.ds(pl.multiple_of(index * chunk, chunk), chunk))
            return carry

        lax.fori_loop(0, width // chunk, one, 0)

    def couple(depth, window):
        value = None
        for i, (a, b) in enumerate(HALF_RING):
            for sign in (1, -1):
                term = times(
                    window(sign * a, sign * b),
                    far[depth, i, 0],
                    far[depth, i, 1],
                    1 if sign > 0 else 0,
                )
                value = term if value is None else value + term
        return value

    def near_and_far(step):
        finish_copies(near_copies(step))
        widen_edges(step)

        def straight(index, columns):
            value = near_term(step, 0, 0, columns)
            for a in (-1, 1):
                value = value + near_term(step, a, 0, columns)
            total[:, columns] = value
            shift_columns(step, -1, index, columns)
            shift_columns(step, 1, index, columns)

        over_columns(straight)

        def sideways(index, columns):
            value = total[:, columns]
            for a in (-1, 0, 1):
                for b in (-1, 1):
                    value = value + near_term(step, a, b, columns)
            total[:, columns] = value

        over_columns(sideways)

        finish_copies(band_copies(step))
        here = []
        span = side
        for depth in range(inner):
            span //= 2
            here.append(
                couple(
                    depth,
                    lambda a, b: bands[depth][
                        step, 1 + a : 1 + a + span, 1 + b : 1 + b + span
                    ].reshape(span * span * 8, 4 * rank),
                )
            )
        finish_gather(*gather_of(step))
        across, along = size_x, size_y
        boxes = gathered[step].reshape(devices * 8, rank)
        for up in range(coarse):
            parents = group(boxes, across, along)
            across, along = across // 2, along // 2
            for i, parent in enumerate(parents):
                tops[up][1 + i // along, 1 + i % along] = parent
            if up < coarse - 1:
                boxes = times(
                    jnp.concatenate(parents, axis=0), lift_high[inner + up], lift_low[inner + up]
                )
        down = None
        for up in range(coarse - 1, -1, -1):
            near_x, near_y = me_x >> up + 1, me_y >> up + 1
            value = couple(
                inner + up, lambda a, b: tops[up][near_x + (1 + a), near_y + (1 + b)]
            )
            if down is not None:
                value = value + times(down, lift_high[inner + up], lift_low[inner + up], 0)
            child = 2 * (me_x >> up & 1) + (me_y >> up & 1)
            down = jnp.zeros((8, rank), F32)
            for i in range(4):
                down = jnp.where(child == i, value[:, i * rank : (i + 1) * rank], down)
        span = 1
        for depth in range(inner - 1, -1, -1):
            value = here[depth] + times(down, lift_high[depth], lift_low[depth], 0)
            if depth > 0:
                down = ungroup(value, span, span)
            span *= 2
        for x in range(side):
            for y in range(side):
                place = pl.ds(x * slab + y, fields, stride=side)
                box = child_of(value, x, y, side // 2)
                skeleton[place, :] = jnp.concatenate([box, box], axis=1)[:fields]
        down = skeleton[0:rows, 0:rank]
        high = down.astype(BF16).astype(F32)
        both = jnp.concatenate([high, down - high], axis=1).astype(BF16)
        total[...] = total[...] + product(both, basis_twice[...])

    for i in (0, 1, 2):
        loads[i].wait()
    skeleton[rows:, :] = jnp.zeros((skeleton.shape[0] - rows, skeleton.shape[1]), F32)
    diagonal = lax.broadcasted_iota(jnp.int32, (side, side), 0) == lax.broadcasted_iota(
        jnp.int32, (side, side), 1
    )

    def begin_first(x, add):
        line = jnp.broadcast_to(occupied[pl.ds(x, 1), :].astype(F32), (side, side))
        column = jnp.sum(jnp.where(diagonal, line, 0.0), axis=1, keepdims=True)
        wide = column * contrast[x]
        weight[x] = wide
        values = {}
        for field, part, place, columns in tiles(x):
            value = rhs[x, field, part]
            add(0, field, value * value)
            values[field, part] = wide * value
            put_product(part, place, values[field, part])
        put_source(0, x, values)

    put_sums(0, sweep(1, begin_first))
    cut_edges(0)
    loads[4].wait()
    loads[5].wait()
    for depth in range(levels - 1):
        lift_high[depth], lift_low[depth] = halves(lifts[depth])
    basis_twice[0:rank] = basis[...]
    basis_twice[rank:] = basis[...]
    upward(0)

    pl.semaphore_wait(barrier, devices - 1)
    start_copies(near_copies(0))
    start_gather(*gather_of(0))
    start_copies(band_copies(0))
    start_gather(*sums_of(0))
    loads[6].wait()

    def build(depth, carry):
        far_level(depth, coupling, far)
        return carry

    lax.fori_loop(0, levels, build, 0)
    loads[3].wait()
    near_and_far(0)

    (square_rhs,) = finish_sums(0, 1)
    beta = jnp.sqrt(square_rhs + EPSILON)
    inverse = 1.0 / beta
    norm_first = square_rhs / (square_rhs + EPSILON)

    by_beta = spread(inverse)

    def begin_second(x, add):
        wide = weight[x] * SHRINK
        values = {}
        for field, part, place, columns in tiles(x):
            value = total[place, columns] * by_beta[field]
            image[place, columns] = value
            add(0, field, rhs[x, field, part] * by_beta[field] * value)
            add(1, field, value * value)
            values[field, part] = wide * value
            put_product(part, place, values[field, part])
        put_source(1, x, values)

    sums = sweep(2, begin_second)
    cut_edges(1)
    start_copies(near_copies(1))
    put_sums(1, sums)
    start_gather(*sums_of(1))
    upward(1)
    start_copies(band_copies(1))
    start_gather(*gather_of(1))
    near_and_far(1)

    along, square = finish_sums(1, 2)
    h11 = norm_first + along
    excess = h11 - 1.0
    square = square - 2.0 * excess * along + excess * excess * norm_first
    h21 = jnp.sqrt(square + EPSILON)
    inverse_second = 1.0 / h21
    norm_second = square / (square + EPSILON)
    cross = (along - excess * norm_first) * inverse_second
    grow, back = inverse_second * (1.0 / SHRINK), -excess * inverse_second

    of_second, by_excess, by_grow = spread(inverse_second), spread(excess), spread(grow)
    by_back = spread(back)

    def moved(x, field, part, place, columns):
        held = image[place, columns]
        return total[place, columns] * by_grow[field] + held * by_back[field]

    def second_sums(x, add):
        for field, part, place, columns in tiles(x):
            first = rhs[x, field, part] * by_beta[field]
            second = (image[place, columns] - by_excess[field] * first) * of_second[field]
            value = moved(x, field, part, place, columns)
            add(0, field, first * value)
            add(1, field, second * value)
            add(2, field, value * value)

    put_sums(2, sweep(3, second_sums))
    start_gather(*sums_of(2))
    on_first, on_second, square = finish_sums(2, 3)
    h12 = cross + on_first
    h22 = norm_second + on_second
    over = h22 - 1.0
    square = (
        square
        + h12 * h12 * norm_first
        + over * over * norm_second
        - 2.0 * h12 * on_first
        - 2.0 * over * on_second
        + 2.0 * h12 * over * cross
    )
    h32 = jnp.sqrt(square + EPSILON)
    inverse_third = 1.0 / h32
    of_total = spread(grow * inverse_third)
    of_image = spread((back - over * inverse_second) * inverse_third)
    of_rhs = spread((over * excess * inverse_second - h12) * inverse_third * inverse)

    def out_copy(x):
        return pltpu.make_async_copy(rhs.at[x], third.at[x], unload.at[x])

    def set_third(x, carry):
        for field, part, place, columns in tiles(x):
            rhs[x, field, part] = (
                total[place, columns] * of_total[field]
                + image[place, columns] * of_image[field]
                + rhs[x, field, part] * of_rhs[field]
            )
        out_copy(x).start()
        return carry

    lax.fori_loop(0, side, set_third, 0)
    tile = jnp.zeros((8, 128), F32)
    for i, column in enumerate([beta, h11, h21, h12, h22, h32]):
        tile = jnp.where(lane == i, column, tile)
    hess[...] = tile
    for x in range(side):
        out_copy(x).wait()


def krylov(rhs, contrast, occupied, near, basis, lifts, coupling, count, size_x, size_y):
    side, fields, comps, _, voxels = rhs.shape
    rank, width = basis.shape
    inner = side.bit_length() - 1
    levels = coupling.shape[0]
    coarse = levels - inner
    devices = size_x * size_y
    slab = fields * side
    rows = side * slab
    ways = len(COMPASS)
    arguments = (rhs, contrast, occupied, near, basis, lifts, coupling)
    scratch = [pltpu.VMEM(value.shape, value.dtype) for value in arguments]
    scratch += [
        pltpu.VMEM((levels, len(HALF_RING), 2, 4 * rank, 4 * rank), BF16),
        pltpu.VMEM((levels - 1, 4 * rank, rank), BF16),
        pltpu.VMEM((levels - 1, 4 * rank, rank), BF16),
        pltpu.VMEM((2 * rank, width), BF16),
        pltpu.VMEM(contrast.shape, F32),
        pltpu.VMEM((width // 128, rows, 128), F32),
        pltpu.VMEM((2, 3, rows + 2 * slab, width), BF16),
        pltpu.VMEM((rows, width), F32),
        pltpu.VMEM((rows, width), F32),
        pltpu.VMEM((rows + 2 * side, 128), F32),
        pltpu.VMEM((2, 2, side * fields, width), BF16),
        pltpu.VMEM((2, 2, side * fields, width), BF16),
        pltpu.VMEM((2, ways, 16, width), BF16),
        pltpu.VMEM((2, side * fields, width), F32),
        pltpu.VMEM((ways, 16, width), F32),
    ]
    for depth in range(inner):
        span = (side >> depth + 1) + 2
        scratch.append(pltpu.VMEM((2, span, span, 8, 4 * rank), F32))
    for up in range(coarse):
        grid = ((size_x >> up + 1) + 2, (size_y >> up + 1) + 2)
        scratch.append(pltpu.VMEM(grid + (8, 4 * rank), F32))
    scratch += [
        pltpu.VMEM((2, 8, rank), F32),
        pltpu.VMEM((2, devices, 8, rank), F32),
        pltpu.VMEM((3, 1, 128), F32),
        pltpu.VMEM((3, devices, 1, 128), F32),
        pltpu.SemaphoreType.DMA((2, ways)),
        pltpu.SemaphoreType.DMA((2, ways)),
        pltpu.SemaphoreType.DMA((inner, 2, ways)),
        pltpu.SemaphoreType.DMA((inner, 2, ways)),
        pltpu.SemaphoreType.DMA((2, devices)),
        pltpu.SemaphoreType.DMA((2, devices)),
        pltpu.SemaphoreType.DMA((3, devices)),
        pltpu.SemaphoreType.DMA((3, devices)),
        pltpu.SemaphoreType.DMA((len(arguments),)),
        pltpu.SemaphoreType.DMA((side,)),
    ]
    anywhere = pl.BlockSpec(memory_space=pl.ANY)
    return pl.pallas_call(
        functools.partial(krylov_kernel, size_x, size_y, inner, count),
        in_specs=[anywhere] * len(arguments),
        out_specs=[anywhere, pl.BlockSpec(memory_space=pltpu.VMEM)],
        out_shape=[
            jax.ShapeDtypeStruct(rhs.shape, F32),
            jax.ShapeDtypeStruct((8, 128), F32),
        ],
        scratch_shapes=scratch,
        compiler_params=pltpu.CompilerParams(collective_id=0, has_side_effects=True),
    )(*arguments)


def body(rhs, contrast, occupied, near, basis, transfer, coupling):
    side, _, fields, parts, voxels = rhs.shape
    rank = basis.shape[1]
    devices_x = lax.axis_size("gx")
    devices_y = lax.axis_size("gy")
    count = float(side * side * devices_x * devices_y * parts * voxels)
    lifts = transfer.reshape(transfer.shape[0], 4 * rank, rank)
    third, hess = krylov(
        rhs.transpose(0, 2, 3, 1, 4),
        contrast,
        occupied,
        near,
        basis.T,
        lifts,
        coupling,
        count,
        devices_x,
        devices_y,
    )
    return (third.transpose(0, 3, 1, 2, 4), hess[:fields, :6])


def solution(mesh):
    placed = (
        P("gx", "gy", None, None, None),
        P("gx", "gy", None),
        P("gx", "gy"),
        P(),
        P(),
        P(),
        P(),
    )
    return jax.shard_map(
        body,
        mesh=mesh,
        in_specs=placed,
        out_specs=(P("gx", "gy", None, None, None), P()),
        check_vma=False,
    )
```

```python
import functools

import jax
import jax.numpy as jnp
from jax import lax
from jax.experimental import pallas as pl
from jax.experimental.pallas import tpu as pltpu
from jax.sharding import PartitionSpec as P

EPSILON = 1e-06
SHRINK = 2.0**-20
NEAR_BASE = ((0, 0), (1, -1), (1, 0), (1, 1), (0, 1))
HALF_RING = NEAR_BASE[1:]
AROUND = [(a, b) for a in (-1, 0, 1) for b in (-1, 0, 1)]
COMPASS = [d for d in AROUND if d != (0, 0)]
CHILDREN = [(c, e) for c in (0, 1) for e in (0, 1)]
MESH = pl.DeviceIdType.MESH
F32 = jnp.float32
BF16 = jnp.bfloat16


def near_lookup():
    table = {}
    for slot, (a, b) in enumerate(NEAR_BASE):
        table[(a, b)] = (slot, False)
        if (a, b) != (0, 0):
            table[(-a, -b)] = (slot, True)
    return table


def far_lookup():
    base = [
        (a, b)
        for a in range(-3, 4)
        for b in range(-3, 4)
        if max(abs(a), abs(b)) >= 2 and (a > 0 or (a == 0 and b > 0))
    ]
    table = {}
    for slot, (a, b) in enumerate(base):
        table[(a, b)] = (slot, False)
        table[(-a, -b)] = (slot, True)
    return table


def halves(values):
    high = values.astype(BF16)
    return high, (values - high.astype(F32)).astype(BF16)


def far_level(depth, coupling, far):
    table = far_lookup()
    rank = coupling.shape[2]
    empty = jnp.zeros((rank, rank), F32)
    seen = {}

    def block_of(offset):
        if offset not in table:
            return empty
        if offset not in seen:
            slot, flipped = table[offset]
            block = coupling[depth, slot]
            seen[offset] = block.T if flipped else block
        return seen[offset]

    for i, (px, py) in enumerate(HALF_RING):
        for k, (c, e) in enumerate(CHILDREN):
            line = [block_of((2 * px + c - tc, 2 * py + e - te)) for tc, te in CHILDREN]
            high, low = halves(jnp.concatenate(line, axis=1))
            far[depth, i, 0, k * rank : (k + 1) * rank, :] = high
            far[depth, i, 1, k * rank : (k + 1) * rank, :] = low


def strip(move, length):
    if move > 0:
        return pl.ds(length, 1), pl.ds(0, 1)
    if move < 0:
        return pl.ds(1, 1), pl.ds(length + 1, 1)
    return pl.ds(1, length), pl.ds(1, length)


def stacked(values):
    high = values.astype(BF16).astype(F32)
    return jnp.concatenate([high, values - high], axis=0).astype(BF16)


def product(left, right, across=1):
    return lax.dot_general(
        left, right, (((1,), (1 - across,)), ((), ())), preferred_element_type=F32
    )


def times(values, high, low, across=1):
    both = stacked(values)
    total = product(both, high, across) + product(both, low, across)
    rows = values.shape[0]
    return total[:rows] + total[rows:]


def group(boxes, size_x, size_y):
    rows = []
    for x in range(0, size_x, 2):
        for y in range(0, size_y, 2):
            four = [(x + c) * size_y + y + e for c, e in CHILDREN]
            rows.append(jnp.concatenate([boxes[8 * i : 8 * i + 8] for i in four], axis=1))
    return rows


def child_of(parents, x, y, size_y):
    rank = parents.shape[1] // 4
    i = (x // 2) * size_y + y // 2
    k = 2 * (x % 2) + y % 2
    return parents[8 * i : 8 * i + 8, k * rank : (k + 1) * rank]


def ungroup(parents, size_x, size_y):
    return jnp.concatenate(
        [child_of(parents, x, y, size_y) for x in range(2 * size_x) for y in range(2 * size_y)],
        axis=0,
    )


def clear_rim(out):
    long_x, long_y = out.shape[0], out.shape[1]
    line_x = jnp.zeros((1,) + out.shape[1:], out.dtype)
    line_y = jnp.zeros((long_x, 1) + out.shape[2:], out.dtype)
    out[0:1] = line_x
    out[long_x - 1 : long_x] = line_x
    out[:, 0:1] = line_y
    out[:, long_y - 1 : long_y] = line_y


def fold(value):
    pieces = [value[:, i : i + 128] for i in range(0, value.shape[1], 128)]
    return functools.reduce(lambda a, b: a + b, pieces)


def krylov_kernel(size_x, size_y, inner, count, *refs):
    arguments, (image_out, total_out, numbers), scratch = refs[:7], refs[7:10], refs[10:]
    rhs, contrast, occupied, near, basis, lifts, coupling = scratch[:7]
    far, lift_high, lift_low, basis_twice, weight, product_of, source = scratch[7:14]
    image, total, skeleton, edge_send, edge, corner, beyond = scratch[14:21]
    bands = scratch[21 : 21 + inner]
    rest = scratch[21 + inner :]
    levels = coupling.shape[0]
    coarse = levels - inner
    tops = rest[:coarse]
    mine, gathered, parts, slots = rest[coarse : coarse + 4]
    near_send, near_receive, band_send, band_receive = rest[coarse + 4 : coarse + 8]
    gather_send, gather_receive, sum_send, sum_receive, load, unload = rest[coarse + 8 :]

    side, fields, comps, _, voxels = rhs.shape
    rank, width = basis.shape
    slab = fields * side
    rows = side * slab
    devices = size_x * size_y
    me_x, me_y = lax.axis_index("gx"), lax.axis_index("gy")
    me = me_x * size_y + me_y
    chunk = 256 if width % 256 == 0 else 128
    lane = lax.broadcasted_iota(jnp.int32, (8, 128), 1)
    sublane = lax.broadcasted_iota(jnp.int32, (8, 128), 0)

    loads = [
        pltpu.make_async_copy(argument, here, load.at[i])
        for i, (argument, here) in enumerate(zip(arguments, scratch[:7]))
    ]
    for i in (0, 1, 2, 4, 5, 6, 3):
        loads[i].start()

    def wrap(value, size):
        return jnp.where(value >= size, value - size, value)

    def others(act):
        def line(shift_x):
            to_x, from_x = wrap(me_x + shift_x, size_x), wrap(me_x + size_x - shift_x, size_x)
            for shift_y in range(size_y):
                if not isinstance(shift_x, int) or (shift_x, shift_y) != (0, 0):
                    to_y = wrap(me_y + shift_y, size_y)
                    from_y = wrap(me_y + size_y - shift_y, size_y)
                    act(shift_x * size_y + shift_y, (to_x, to_y), from_x * size_y + from_y)

        if devices <= 64:
            for shift_x in range(size_x):
                line(shift_x)
        else:
            line(0)

            def one(shift_x, carry):
                line(shift_x)
                return carry

            lax.fori_loop(1, size_x, one, 0)

    for step in (0, 1):
        for side_rows in (slice(0, slab), slice((side + 1) * slab, (side + 2) * slab)):
            source[step, 1, side_rows] = jnp.zeros((slab, width), BF16)
        edge[step] = jnp.zeros(edge.shape[1:], BF16)
        corner[step] = jnp.zeros(corner.shape[1:], BF16)
        for band in bands:
            clear_rim(band.at[step])
    for top in tops:
        clear_rim(top)

    barrier = pltpu.get_barrier_semaphore()

    def greet(step, to, before):
        pl.semaphore_signal(
            barrier, inc=1, device_id={"gx": to[0], "gy": to[1]}, device_id_type=MESH
        )

    others(greet)

    def gather_copy(piece, target, sent, received, step, to, slot):
        return pltpu.make_async_remote_copy(
            src_ref=piece,
            dst_ref=target.at[slot],
            send_sem=sent.at[step],
            recv_sem=received.at[step],
            device_id={"gx": to[0], "gy": to[1]},
            device_id_type=MESH,
        )

    def start_gather(*what):
        others(lambda step, to, before: gather_copy(*what, step, to, me).start())

    def finish_gather(*what):
        others(lambda step, to, before: gather_copy(*what, step, to, before).wait())

    def sums_of(number):
        return parts.at[number], slots.at[number], sum_send.at[number], sum_receive.at[number]

    def put_sums(number, sums):
        tile = jnp.zeros((8, 128), F32)
        for i, of_fields in enumerate(sums):
            lines = [jnp.sum(value, axis=0, keepdims=True) for value in of_fields]
            lines.append(jnp.zeros((8 - fields, 128), F32))
            column = jnp.sum(jnp.concatenate(lines, axis=0), axis=1, keepdims=True)
            tile = tile + jnp.where(lane == 8 * i + sublane, column, 0.0)
        line = jnp.sum(tile, axis=0, keepdims=True)
        parts[number] = line
        slots[number, me] = line

    def finish_sums(number, amount):
        finish_gather(*sums_of(number))
        line = jnp.broadcast_to(jnp.sum(slots[number], axis=0) * (1.0 / count), (8, 128))
        return [
            jnp.sum(jnp.where(lane == 8 * i + sublane, line, 0.0), axis=1, keepdims=True)
            for i in range(amount)
        ]

    def spread(column):
        return [
            jnp.broadcast_to(column[field : field + 1, :], (8, voxels)) for field in range(fields)
        ]

    def sweep(amount, work):
        zero = tuple(jnp.zeros((8, 128), F32) for _ in range(amount * fields))

        def one(x, sums):
            sums = [list(sums[i * fields : (i + 1) * fields]) for i in range(amount)]

            def add(i, field, value):
                sums[i][field] = sums[i][field] + fold(value)

            work(x, add)
            return tuple(value for of_fields in sums for value in of_fields)

        out = lax.fori_loop(0, side, one, zero)
        return [out[i * fields : (i + 1) * fields] for i in range(amount)]

    def tiles(x):
        for field in range(fields):
            place = pl.ds(pl.multiple_of(x * slab + field * side, 8), side)
            for part in range(comps):
                yield field, part, place

    def put(target, begin, place, value):
        for i in range(value.shape[1] // 128):
            target[begin + i, place] = value[:, i * 128 : (i + 1) * 128]

    def get(target, begin, place, amount):
        return jnp.concatenate([target[begin + i, place] for i in range(amount)], axis=1)

    splits = voxels // 128

    def put_source(step, x, values):
        for field in range(0, fields, 2):
            place = pl.ds(pl.multiple_of((x + 1) * slab + field * side, 16), 2 * side)
            for part in range(comps):
                pair = [values[field + i, part] for i in (0, 1)]
                columns = slice(part * voxels, (part + 1) * voxels)
                source[step, 1, place, columns] = jnp.concatenate(pair, axis=0).astype(BF16)

    def inside(place_x, place_y):
        return (place_x >= 0) & (place_x < size_x) & (place_y >= 0) & (place_y < size_y)

    def near_copy(step, way):
        move_x, move_y = COMPASS[way]
        if move_y == 0:
            begin, end = (side, 0) if move_x > 0 else (1, side + 1)
            from_ref = source.at[step, 1, pl.ds(begin * slab, slab)]
            to_ref = source.at[step, 1, pl.ds(end * slab, slab)]
        else:
            from_ref = edge_send.at[step, int(move_y > 0)]
            to_ref = edge.at[step, int(move_y > 0)]
            if move_x != 0:
                begin = from_ref.shape[0] - 16 if move_x > 0 else 0
                from_ref, to_ref = from_ref.at[pl.ds(begin, 16)], corner.at[step, way]
        return pltpu.make_async_remote_copy(
            src_ref=from_ref,
            dst_ref=to_ref,
            send_sem=near_send.at[step, way],
            recv_sem=near_receive.at[step, way],
            device_id={"gx": me_x + move_x, "gy": me_y + move_y},
            device_id_type=MESH,
        )

    def band_copy(number, step, way):
        move_x, move_y = COMPASS[way]
        band = bands[number].at[step]
        from_x, to_x = strip(move_x, band.shape[0] - 2)
        from_y, to_y = strip(move_y, band.shape[1] - 2)
        return pltpu.make_async_remote_copy(
            src_ref=band.at[from_x, from_y],
            dst_ref=band.at[to_x, to_y],
            send_sem=band_send.at[number, step, way],
            recv_sem=band_receive.at[number, step, way],
            device_id={"gx": me_x + move_x, "gy": me_y + move_y},
            device_id_type=MESH,
        )

    def near_copies(step):
        return [functools.partial(near_copy, step)]

    def band_copies(step):
        return [functools.partial(band_copy, number, step) for number in range(inner)]

    def start_copies(copies):
        for way, (move_x, move_y) in enumerate(COMPASS):

            @pl.when(inside(me_x + move_x, me_y + move_y))
            def _(way=way):
                for copy in copies:
                    copy(way).start()

    def finish_copies(copies, wanted=lambda move_y: True):
        for way, (move_x, move_y) in enumerate(COMPASS):
            if not wanted(move_y):
                continue

            @pl.when(inside(me_x + move_x, me_y + move_y))
            def _(way=way):
                for copy in copies:
                    copy(way).wait_send()

            @pl.when(inside(me_x - move_x, me_y - move_y))
            def _(way=way):
                for copy in copies:
                    copy(way).wait_recv()

    def cut_edges(step):
        for i, y in enumerate((0, side - 1)):
            for part in range(width // 128):
                line = product_of[part, pl.ds(y, side * fields, stride=side), :]
                edge_send[step, i, :, part * 128 : (part + 1) * 128] = line.astype(BF16)

    def upward(step):
        own = source[step, 1, slab : slab + rows]
        skeleton[0:rows, 0:rank] = product(own, basis[...], 0)
        parents = []
        for x in range(0, side, 2):
            for y in range(0, side, 2):
                four = [
                    skeleton[pl.ds((x + c) * slab + y + e, 8, stride=side), :][:, :rank]
                    for c, e in CHILDREN
                ]
                parents.append(jnp.concatenate(four, axis=1))
        span = side
        for depth in range(inner):
            span //= 2
            for i, parent in enumerate(parents):
                bands[depth][step, 1 + i // span, 1 + i % span] = parent
            level = times(jnp.concatenate(parents, axis=0), lift_high[depth], lift_low[depth])
            if depth < inner - 1:
                parents = group(level, span, span)
        mine[step] = level
        gathered[step, me] = level

    def gather_of(step):
        return mine.at[step], gathered.at[step], gather_send.at[step], gather_receive.at[step]

    table = near_lookup()

    def near_term(step, a, b, columns):
        piece = source[step, 1 + b, (1 + a) * slab : (1 + a) * slab + rows]
        return near_product(a, b, piece, columns)

    def near_product(a, b, piece, columns):
        slot, flipped = table[(a, b)]
        if flipped:
            return product(piece, near[slot, columns, :], 0)
        return product(piece, near[slot, :, columns])

    pieces = chunk // 128
    row_of = lax.broadcasted_iota(jnp.int32, (side, chunk), 0)

    def shift_rows(step, b, x, own, columns):
        shifted = []
        for field in range(fields):
            value = own[field * side : (field + 1) * side]
            value = pltpu.roll(value, side - 1 if b > 0 else 1, 0)
            shifted.append(jnp.where(row_of == (side - 1 if b > 0 else 0), 0.0, value))
        for field in range(0, fields, 2):
            begin = (x + 1) * slab + field * side
            source[step, 1 + b, begin : begin + 2 * side, columns] = jnp.concatenate(
                shifted[field : field + 2], axis=0
            ).astype(BF16)

    def over_columns(work):
        def one(index, carry):
            work(index, pl.ds(pl.multiple_of(index * chunk, chunk), chunk))
            return carry

        lax.fori_loop(0, width // chunk, one, 0)

    def couple(depth, window):
        value = None
        for i, (a, b) in enumerate(HALF_RING):
            for sign in (1, -1):
                term = times(
                    window(sign * a, sign * b),
                    far[depth, i, 0],
                    far[depth, i, 1],
                    1 if sign > 0 else 0,
                )
                value = term if value is None else value + term
        return value

    def near_local(step):
        def straight(index, columns):
            put(total, index * pieces, slice(0, rows), near_term(step, 0, 0, columns))
            for x in range(side):
                own = get(product_of, index * pieces, slice(x * slab, (x + 1) * slab), pieces)
                shift_rows(step, -1, x, own, columns)
                shift_rows(step, 1, x, own, columns)

        over_columns(straight)

        def level(index, columns):
            value = get(total, index * pieces, slice(0, rows), pieces)
            for b in (-1, 1):
                value = value + near_term(step, 0, b, columns)
            put(total, index * pieces, slice(0, rows), value)

        over_columns(level)

    def beyond_edges(step):
        finish_copies(near_copies(step), lambda move_y: move_y != 0)
        last = fields * (side + 1)
        for i, b in enumerate((1, -1)):
            low, high = COMPASS.index((1, -b)), COMPASS.index((-1, -b))
            beyond[i, 0:fields] = corner[step, low].astype(F32)[16 - fields :]
            beyond[i, fields:last] = edge[step, i].astype(F32)
            beyond[i, last : last + fields] = corner[step, high].astype(F32)[:fields]

        def one(index, columns):
            for i, b in enumerate((1, -1)):
                value = None
                for a in (-1, 0, 1):
                    begin = (1 + a) * fields
                    piece = beyond[i, begin : begin + fields * side].astype(BF16)
                    term = near_product(a, b, piece, columns)
                    value = term if value is None else value + term
                place = pl.ds(side - 1 if b > 0 else 0, fields * side, stride=side)
                old = get(total, index * pieces, place, pieces)
                put(total, index * pieces, place, old + value)

        over_columns(one)

    def near_and_far(step):
        finish_copies(near_copies(step), lambda move_y: move_y == 0)
        for x in (-1, side):
            for begin in range(0, width, chunk):
                columns = slice(begin, begin + chunk)
                own = source[step, 1, (x + 1) * slab : (x + 2) * slab, columns].astype(F32)
                shift_rows(step, -1, x, own, columns)
                shift_rows(step, 1, x, own, columns)

        def sideways(index, columns):
            value = get(total, index * pieces, slice(0, rows), pieces)
            for a in (-1, 1):
                for b in (-1, 0, 1):
                    value = value + near_term(step, a, b, columns)
            put(total, index * pieces, slice(0, rows), value)

        over_columns(sideways)
        finish_copies(band_copies(step))
        here = []
        span = side
        for depth in range(inner):
            span //= 2
            here.append(
                couple(
                    depth,
                    lambda a, b: bands[depth][
                        step, 1 + a : 1 + a + span, 1 + b : 1 + b + span
                    ].reshape(span * span * 8, 4 * rank),
                )
            )
        beyond_edges(step)
        finish_gather(*gather_of(step))
        across, along = size_x, size_y
        boxes = gathered[step].reshape(devices * 8, rank)
        for up in range(coarse):
            parents = group(boxes, across, along)
            across, along = across // 2, along // 2
            for i, parent in enumerate(parents):
                tops[up][1 + i // along, 1 + i % along] = parent
            if up < coarse - 1:
                boxes = times(
                    jnp.concatenate(parents, axis=0), lift_high[inner + up], lift_low[inner + up]
                )
        down = None
        for up in range(coarse - 1, -1, -1):
            near_x, near_y = me_x >> up + 1, me_y >> up + 1
            value = couple(
                inner + up, lambda a, b: tops[up][near_x + (1 + a), near_y + (1 + b)]
            )
            if down is not None:
                value = value + times(down, lift_high[inner + up], lift_low[inner + up], 0)
            child = 2 * (me_x >> up & 1) + (me_y >> up & 1)
            down = jnp.zeros((8, rank), F32)
            for i in range(4):
                down = jnp.where(child == i, value[:, i * rank : (i + 1) * rank], down)
        span = 1
        for depth in range(inner - 1, -1, -1):
            value = here[depth] + times(down, lift_high[depth], lift_low[depth], 0)
            if depth > 0:
                down = ungroup(value, span, span)
            span *= 2
        for x in range(side):
            for y in range(side):
                place = pl.ds(x * slab + y, fields, stride=side)
                box = child_of(value, x, y, side // 2)
                skeleton[place, :] = jnp.concatenate([box, box], axis=1)[:fields]
        down = skeleton[0:rows, 0:rank]
        high = down.astype(BF16).astype(F32)
        both = jnp.concatenate([high, down - high], axis=1).astype(BF16)
        for begin in range(0, width, 256):
            value = product(both, basis_twice[:, begin : begin + 256])
            amount = value.shape[1] // 128
            everywhere = slice(0, rows)
            put(total, begin // 128, everywhere, get(total, begin // 128, everywhere, amount) + value)

    for i in (0, 1, 2):
        loads[i].wait()
    skeleton[rows:, :] = jnp.zeros((skeleton.shape[0] - rows, skeleton.shape[1]), F32)
    diagonal = lax.broadcasted_iota(jnp.int32, (side, side), 0) == lax.broadcasted_iota(
        jnp.int32, (side, side), 1
    )

    def begin_first(x, add):
        line = jnp.broadcast_to(occupied[pl.ds(x, 1), :].astype(F32), (side, side))
        column = jnp.sum(jnp.where(diagonal, line, 0.0), axis=1, keepdims=True)
        wide = column * contrast[x]
        weight[x] = wide
        values = {}
        for field, part, place in tiles(x):
            value = rhs[x, field, part]
            add(0, field, value * value)
            values[field, part] = wide * value
            put(product_of, part * splits, place, values[field, part])
        put_source(0, x, values)

    put_sums(0, sweep(1, begin_first))
    cut_edges(0)
    loads[4].wait()
    loads[5].wait()
    for depth in range(levels - 1):
        lift_high[depth], lift_low[depth] = halves(lifts[depth])
    basis_twice[0:rank] = basis[...]
    basis_twice[rank:] = basis[...]
    upward(0)

    loads[3].wait()
    near_local(0)

    pl.semaphore_wait(barrier, devices - 1)
    start_copies(near_copies(0))
    start_copies(band_copies(0))
    start_gather(*gather_of(0))
    start_gather(*sums_of(0))
    loads[6].wait()

    def build(depth, carry):
        far_level(depth, coupling, far)
        return carry

    lax.fori_loop(0, levels, build, 0)
    near_and_far(0)

    (square_rhs,) = finish_sums(0, 1)
    beta = jnp.sqrt(square_rhs + EPSILON)
    inverse = 1.0 / beta
    norm_first = square_rhs / (square_rhs + EPSILON)

    by_beta = spread(inverse)

    def begin_second(x, add):
        wide = weight[x] * SHRINK
        values = {}
        for field, part, place in tiles(x):
            value = get(total, part * splits, place, splits) * by_beta[field]
            put(image, part * splits, place, value)
            add(0, field, rhs[x, field, part] * by_beta[field] * value)
            add(1, field, value * value)
            values[field, part] = wide * value
            put(product_of, part * splits, place, values[field, part])
        put_source(1, x, values)

    sums = sweep(2, begin_second)
    cut_edges(1)
    start_copies(near_copies(1))
    image_copy = pltpu.make_async_copy(image, image_out, unload.at[0])
    image_copy.start()
    upward(1)
    start_copies(band_copies(1))
    start_gather(*gather_of(1))
    put_sums(1, sums)
    start_gather(*sums_of(1))
    near_local(1)
    near_and_far(1)
    total_copy = pltpu.make_async_copy(total, total_out, unload.at[1])
    total_copy.start()

    along, square = finish_sums(1, 2)
    h11 = norm_first + along
    excess = h11 - 1.0
    square = square - 2.0 * excess * along + excess * excess * norm_first
    h21 = jnp.sqrt(square + EPSILON)
    inverse_second = 1.0 / h21
    norm_second = square / (square + EPSILON)
    cross = (along - excess * norm_first) * inverse_second
    grow, back = inverse_second * (1.0 / SHRINK), -excess * inverse_second

    of_second, by_excess, by_grow = spread(inverse_second), spread(excess), spread(grow)
    by_back = spread(back)

    def second_sums(x, add):
        for field, part, place in tiles(x):
            first = rhs[x, field, part] * by_beta[field]
            held = get(image, part * splits, place, splits)
            second = (held - by_excess[field] * first) * of_second[field]
            value = get(total, part * splits, place, splits) * by_grow[field]
            value = value + held * by_back[field]
            add(0, field, first * value)
            add(1, field, second * value)
            add(2, field, value * value)

    put_sums(2, sweep(3, second_sums))
    start_gather(*sums_of(2))
    on_first, on_second, square = finish_sums(2, 3)
    h12 = cross + on_first
    h22 = norm_second + on_second
    over = h22 - 1.0
    square = (
        square
        + h12 * h12 * norm_first
        + over * over * norm_second
        - 2.0 * h12 * on_first
        - 2.0 * over * on_second
        + 2.0 * h12 * over * cross
    )
    h32 = jnp.sqrt(square + EPSILON)
    inverse_third = 1.0 / h32
    columns = [beta, h11, h21, h12, h22, h32]
    columns.append(grow * inverse_third)
    columns.append((back - over * inverse_second) * inverse_third)
    columns.append((over * excess * inverse_second - h12) * inverse_third * inverse)
    tile = jnp.zeros((8, 128), F32)
    for i, column in enumerate(columns):
        tile = jnp.where(lane == i, column, tile)
    numbers[...] = tile
    image_copy.wait()
    total_copy.wait()


def combine_kernel(rhs, image, total, numbers, third, hess):
    deep, fields, comps, side, voxels = rhs.shape
    splits = voxels // 128
    hess[...] = numbers[:fields, :6]
    for field in range(fields):
        of_total, of_image, of_rhs = [
            jnp.broadcast_to(numbers[field : field + 1, i : i + 1], (side, 128)) for i in (6, 7, 8)
        ]
        for x in range(deep):
            place = slice((x * fields + field) * side, (x * fields + field + 1) * side)
            for part in range(comps):
                for i in range(splits):
                    at = part * splits + i
                    lanes = slice(i * 128, (i + 1) * 128)
                    third[x, field, part, :, lanes] = (
                        total[at, place] * of_total
                        + image[at, place] * of_image
                        + rhs[x, field, part, :, lanes] * of_rhs
                    )


def combine(rhs, image, total, numbers):
    side, fields, comps, _, voxels = rhs.shape
    deep = 2 if side % 2 == 0 else 1
    block = (deep,) + rhs.shape[1:]
    lines = deep * fields * side
    whole = lambda shape: pl.BlockSpec(shape, lambda i: (0, 0))
    slabs = pl.BlockSpec((image.shape[0], lines, 128), lambda i: (0, i, 0))
    boxes = pl.BlockSpec(block, lambda i: (i, 0, 0, 0, 0))
    return pl.pallas_call(
        combine_kernel,
        grid=(side // deep,),
        in_specs=[boxes, slabs, slabs, whole(numbers.shape)],
        out_specs=[boxes, whole((fields, 6))],
        out_shape=[
            jax.ShapeDtypeStruct(rhs.shape, F32),
            jax.ShapeDtypeStruct((fields, 6), F32),
        ],
    )(rhs, image, total, numbers)


def krylov(rhs, contrast, occupied, near, basis, lifts, coupling, count, size_x, size_y):
    side, fields, comps, _, voxels = rhs.shape
    rank, width = basis.shape
    inner = side.bit_length() - 1
    levels = coupling.shape[0]
    coarse = levels - inner
    devices = size_x * size_y
    slab = fields * side
    rows = side * slab
    ways = len(COMPASS)
    arguments = (rhs, contrast, occupied, near, basis, lifts, coupling)
    scratch = [pltpu.VMEM(value.shape, value.dtype) for value in arguments]
    scratch += [
        pltpu.VMEM((levels, len(HALF_RING), 2, 4 * rank, 4 * rank), BF16),
        pltpu.VMEM((levels - 1, 4 * rank, rank), BF16),
        pltpu.VMEM((levels - 1, 4 * rank, rank), BF16),
        pltpu.VMEM((2 * rank, width), BF16),
        pltpu.VMEM(contrast.shape, F32),
        pltpu.VMEM((width // 128, rows, 128), F32),
        pltpu.VMEM((2, 3, rows + 2 * slab, width), BF16),
        pltpu.VMEM((width // 128, rows, 128), F32),
        pltpu.VMEM((width // 128, rows, 128), F32),
        pltpu.VMEM((rows + 2 * side, 128), F32),
        pltpu.VMEM((2, 2, side * fields, width), BF16),
        pltpu.VMEM((2, 2, side * fields, width), BF16),
        pltpu.VMEM((2, ways, 16, width), BF16),
        pltpu.VMEM((2, (side + 3) * fields, width), F32),
    ]
    for depth in range(inner):
        span = (side >> depth + 1) + 2
        scratch.append(pltpu.VMEM((2, span, span, 8, 4 * rank), F32))
    for up in range(coarse):
        grid = ((size_x >> up + 1) + 2, (size_y >> up + 1) + 2)
        scratch.append(pltpu.VMEM(grid + (8, 4 * rank), F32))
    scratch += [
        pltpu.VMEM((2, 8, rank), F32),
        pltpu.VMEM((2, devices, 8, rank), F32),
        pltpu.VMEM((3, 1, 128), F32),
        pltpu.VMEM((3, devices, 1, 128), F32),
        pltpu.SemaphoreType.DMA((2, ways)),
        pltpu.SemaphoreType.DMA((2, ways)),
        pltpu.SemaphoreType.DMA((inner, 2, ways)),
        pltpu.SemaphoreType.DMA((inner, 2, ways)),
        pltpu.SemaphoreType.DMA((2, devices)),
        pltpu.SemaphoreType.DMA((2, devices)),
        pltpu.SemaphoreType.DMA((3, devices)),
        pltpu.SemaphoreType.DMA((3, devices)),
        pltpu.SemaphoreType.DMA((len(arguments),)),
        pltpu.SemaphoreType.DMA((2,)),
    ]
    anywhere = pl.BlockSpec(memory_space=pl.ANY)
    return pl.pallas_call(
        functools.partial(krylov_kernel, size_x, size_y, inner, count),
        in_specs=[anywhere] * len(arguments),
        out_specs=[anywhere, anywhere, pl.BlockSpec(memory_space=pltpu.VMEM)],
        out_shape=[
            jax.ShapeDtypeStruct((width // 128, rows, 128), F32),
            jax.ShapeDtypeStruct((width // 128, rows, 128), F32),
            jax.ShapeDtypeStruct((8, 128), F32),
        ],
        scratch_shapes=scratch,
        compiler_params=pltpu.CompilerParams(collective_id=0, has_side_effects=True),
    )(*arguments)


def body(rhs, contrast, occupied, near, basis, transfer, coupling):
    side, _, _, parts, voxels = rhs.shape
    rank = basis.shape[1]
    devices_x = lax.axis_size("gx")
    devices_y = lax.axis_size("gy")
    count = float(side * side * devices_x * devices_y * parts * voxels)
    lifts = transfer.reshape(transfer.shape[0], 4 * rank, rank)
    flat = rhs.transpose(0, 2, 3, 1, 4)
    image, total, numbers = krylov(
        flat,
        contrast,
        occupied,
        near,
        basis.T,
        lifts,
        coupling,
        count,
        devices_x,
        devices_y,
    )
    third, hess = combine(flat, image, total, numbers)
    return (third.transpose(0, 3, 1, 2, 4), hess)


def solution(mesh):
    placed = (
        P("gx", "gy", None, None, None),
        P("gx", "gy", None),
        P("gx", "gy"),
        P(),
        P(),
        P(),
        P(),
    )
    return jax.shard_map(
        body,
        mesh=mesh,
        in_specs=placed,
        out_specs=(P("gx", "gy", None, None, None), P()),
        check_vma=False,
    )
```

```python
import functools

import jax
import jax.numpy as jnp
from jax import lax
from jax.experimental import pallas as pl
from jax.experimental.pallas import tpu as pltpu
from jax.sharding import PartitionSpec as P

EPSILON = 1e-06
SHRINK = 2.0**-20
NEAR_BASE = ((0, 0), (1, -1), (1, 0), (1, 1), (0, 1))
HALF_RING = NEAR_BASE[1:]
AROUND = [(a, b) for a in (-1, 0, 1) for b in (-1, 0, 1)]
COMPASS = [d for d in AROUND if d != (0, 0)]
CHILDREN = [(c, e) for c in (0, 1) for e in (0, 1)]
MESH = pl.DeviceIdType.MESH
F32 = jnp.float32
BF16 = jnp.bfloat16


def near_lookup():
    table = {}
    for slot, (a, b) in enumerate(NEAR_BASE):
        table[(a, b)] = (slot, False)
        if (a, b) != (0, 0):
            table[(-a, -b)] = (slot, True)
    return table


def far_lookup():
    base = [
        (a, b)
        for a in range(-3, 4)
        for b in range(-3, 4)
        if max(abs(a), abs(b)) >= 2 and (a > 0 or (a == 0 and b > 0))
    ]
    table = {}
    for slot, (a, b) in enumerate(base):
        table[(a, b)] = (slot, False)
        table[(-a, -b)] = (slot, True)
    return table


def halves(values):
    high = values.astype(BF16)
    return high, (values - high.astype(F32)).astype(BF16)


def far_level(depth, coupling, far):
    table = far_lookup()
    rank = coupling.shape[2]
    empty = jnp.zeros((rank, rank), F32)
    seen = {}

    def block_of(offset):
        if offset not in table:
            return empty
        if offset not in seen:
            slot, flipped = table[offset]
            block = coupling[depth, slot]
            seen[offset] = block.T if flipped else block
        return seen[offset]

    for i, (px, py) in enumerate(HALF_RING):
        for k, (c, e) in enumerate(CHILDREN):
            line = [block_of((2 * px + c - tc, 2 * py + e - te)) for tc, te in CHILDREN]
            high, low = halves(jnp.concatenate(line, axis=1))
            far[depth, i, 0, k * rank : (k + 1) * rank, :] = high
            far[depth, i, 1, k * rank : (k + 1) * rank, :] = low


def strip(move, length):
    if move > 0:
        return pl.ds(length, 1), pl.ds(0, 1)
    if move < 0:
        return pl.ds(1, 1), pl.ds(length + 1, 1)
    return pl.ds(1, length), pl.ds(1, length)


def stacked(values):
    high = values.astype(BF16).astype(F32)
    return jnp.concatenate([high, values - high], axis=0).astype(BF16)


def product(left, right, across=1):
    return lax.dot_general(
        left, right, (((1,), (1 - across,)), ((), ())), preferred_element_type=F32
    )


def times(values, high, low, across=1):
    both = stacked(values)
    total = product(both, high, across) + product(both, low, across)
    rows = values.shape[0]
    return total[:rows] + total[rows:]


def group(boxes, size_x, size_y):
    rows = []
    for x in range(0, size_x, 2):
        for y in range(0, size_y, 2):
            four = [(x + c) * size_y + y + e for c, e in CHILDREN]
            rows.append(jnp.concatenate([boxes[8 * i : 8 * i + 8] for i in four], axis=1))
    return rows


def child_of(parents, x, y, size_y):
    rank = parents.shape[1] // 4
    i = (x // 2) * size_y + y // 2
    k = 2 * (x % 2) + y % 2
    return parents[8 * i : 8 * i + 8, k * rank : (k + 1) * rank]


def ungroup(parents, size_x, size_y):
    return jnp.concatenate(
        [child_of(parents, x, y, size_y) for x in range(2 * size_x) for y in range(2 * size_y)],
        axis=0,
    )


def clear_rim(out):
    long_x, long_y = out.shape[0], out.shape[1]
    line_x = jnp.zeros((1,) + out.shape[1:], out.dtype)
    line_y = jnp.zeros((long_x, 1) + out.shape[2:], out.dtype)
    out[0:1] = line_x
    out[long_x - 1 : long_x] = line_x
    out[:, 0:1] = line_y
    out[:, long_y - 1 : long_y] = line_y


def fold(value):
    pieces = [value[:, i : i + 128] for i in range(0, value.shape[1], 128)]
    return functools.reduce(lambda a, b: a + b, pieces)


def krylov_kernel(size_x, size_y, inner, count, *refs):
    arguments, (image_out, total_out, numbers), scratch = refs[:7], refs[7:10], refs[10:]
    rhs, contrast, occupied, near, basis, lifts, coupling = scratch[:7]
    far, lift_high, lift_low, basis_twice, weight, product_of, source = scratch[7:14]
    image, total, skeleton, edge_send, edge, corner, beyond = scratch[14:21]
    bands = scratch[21 : 21 + inner]
    rest = scratch[21 + inner :]
    levels = coupling.shape[0]
    coarse = levels - inner
    tops = rest[:coarse]
    mine, gathered, parts, slots = rest[coarse : coarse + 4]
    near_send, near_receive, band_send, band_receive = rest[coarse + 4 : coarse + 8]
    gather_send, gather_receive, sum_send, sum_receive, load, unload = rest[coarse + 8 :]

    side, fields, comps, _, voxels = rhs.shape
    rank, width = basis.shape
    slab = fields * side
    rows = side * slab
    devices = size_x * size_y
    me_x, me_y = lax.axis_index("gx"), lax.axis_index("gy")
    me = me_x * size_y + me_y
    chunk = 256 if width % 256 == 0 else 128
    lane = lax.broadcasted_iota(jnp.int32, (8, 128), 1)
    sublane = lax.broadcasted_iota(jnp.int32, (8, 128), 0)

    loads = [
        pltpu.make_async_copy(argument, here, load.at[i])
        for i, (argument, here) in enumerate(zip(arguments, scratch[:7]))
    ]
    for i in (0, 1, 2, 4, 5, 6, 3):
        loads[i].start()

    def wrap(value, size):
        return jnp.where(value >= size, value - size, value)

    def others(act):
        def line(shift_x):
            to_x, from_x = wrap(me_x + shift_x, size_x), wrap(me_x + size_x - shift_x, size_x)
            for shift_y in range(size_y):
                if not isinstance(shift_x, int) or (shift_x, shift_y) != (0, 0):
                    to_y = wrap(me_y + shift_y, size_y)
                    from_y = wrap(me_y + size_y - shift_y, size_y)
                    act(shift_x * size_y + shift_y, (to_x, to_y), from_x * size_y + from_y)

        if devices <= 64:
            for shift_x in range(size_x):
                line(shift_x)
        else:
            line(0)

            def one(shift_x, carry):
                line(shift_x)
                return carry

            lax.fori_loop(1, size_x, one, 0)

    for step in (0, 1):
        for side_rows in (slice(0, slab), slice((side + 1) * slab, (side + 2) * slab)):
            source[step, 1, side_rows] = jnp.zeros((slab, width), BF16)
        edge[step] = jnp.zeros(edge.shape[1:], BF16)
        corner[step] = jnp.zeros(corner.shape[1:], BF16)
        for band in bands:
            clear_rim(band.at[step])
    for top in tops:
        clear_rim(top)

    barrier = pltpu.get_barrier_semaphore()

    def greet(step, to, before):
        pl.semaphore_signal(
            barrier, inc=1, device_id={"gx": to[0], "gy": to[1]}, device_id_type=MESH
        )

    others(greet)

    def gather_copy(piece, target, sent, received, to, slot):
        return pltpu.make_async_remote_copy(
            src_ref=piece,
            dst_ref=target.at[slot],
            send_sem=sent,
            recv_sem=received,
            device_id={"gx": to[0], "gy": to[1]},
            device_id_type=MESH,
        )

    def start_gather(*what):
        others(lambda step, to, before: gather_copy(*what, to, me).start())

    def finish_gather(piece, target, sent, received):
        bulk = target.at[pl.ds(0, devices - 1)]
        pltpu.make_async_copy(bulk, bulk, received).wait()
        pltpu.make_async_copy(bulk, bulk, sent).wait()

    def sums_of(number):
        return parts.at[number], slots.at[number], sum_send.at[number], sum_receive.at[number]

    def put_sums(number, sums):
        tile = jnp.zeros((8, 128), F32)
        for i, of_fields in enumerate(sums):
            lines = [jnp.sum(value, axis=0, keepdims=True) for value in of_fields]
            lines.append(jnp.zeros((8 - fields, 128), F32))
            column = jnp.sum(jnp.concatenate(lines, axis=0), axis=1, keepdims=True)
            tile = tile + jnp.where(lane == 8 * i + sublane, column, 0.0)
        line = jnp.sum(tile, axis=0, keepdims=True)
        parts[number] = line
        slots[number, me] = line

    def finish_sums(number, amount):
        finish_gather(*sums_of(number))
        line = jnp.broadcast_to(jnp.sum(slots[number], axis=0) * (1.0 / count), (8, 128))
        return [
            jnp.sum(jnp.where(lane == 8 * i + sublane, line, 0.0), axis=1, keepdims=True)
            for i in range(amount)
        ]

    def spread(column):
        return [
            jnp.broadcast_to(column[field : field + 1, :], (8, voxels)) for field in range(fields)
        ]

    def sweep(amount, work):
        zero = tuple(jnp.zeros((8, 128), F32) for _ in range(amount * fields))

        def one(x, sums):
            sums = [list(sums[i * fields : (i + 1) * fields]) for i in range(amount)]

            def add(i, field, value):
                sums[i][field] = sums[i][field] + fold(value)

            work(x, add)
            return tuple(value for of_fields in sums for value in of_fields)

        out = lax.fori_loop(0, side, one, zero)
        return [out[i * fields : (i + 1) * fields] for i in range(amount)]

    def tiles(x):
        for field in range(fields):
            place = pl.ds(pl.multiple_of(x * slab + field * side, 8), side)
            for part in range(comps):
                yield field, part, place

    def put(target, begin, place, value):
        for i in range(value.shape[1] // 128):
            target[begin + i, place] = value[:, i * 128 : (i + 1) * 128]

    def get(target, begin, place, amount):
        return jnp.concatenate([target[begin + i, place] for i in range(amount)], axis=1)

    splits = voxels // 128

    def put_source(step, x, values):
        for field in range(0, fields, 2):
            place = pl.ds(pl.multiple_of((x + 1) * slab + field * side, 16), 2 * side)
            for part in range(comps):
                pair = [values[field + i, part] for i in (0, 1)]
                columns = slice(part * voxels, (part + 1) * voxels)
                source[step, 1, place, columns] = jnp.concatenate(pair, axis=0).astype(BF16)

    def inside(place_x, place_y):
        return (place_x >= 0) & (place_x < size_x) & (place_y >= 0) & (place_y < size_y)

    def near_copy(step, way):
        move_x, move_y = COMPASS[way]
        if move_y == 0:
            begin, end = (side, 0) if move_x > 0 else (1, side + 1)
            from_ref = source.at[step, 1, pl.ds(begin * slab, slab)]
            to_ref = source.at[step, 1, pl.ds(end * slab, slab)]
        else:
            from_ref = edge_send.at[step, int(move_y > 0)]
            to_ref = edge.at[step, int(move_y > 0)]
            if move_x != 0:
                begin = from_ref.shape[0] - 16 if move_x > 0 else 0
                from_ref, to_ref = to_ref.at[pl.ds(begin, 16)], corner.at[step, way]
                move_y = 0
        return pltpu.make_async_remote_copy(
            src_ref=from_ref,
            dst_ref=to_ref,
            send_sem=near_send.at[step, way],
            recv_sem=near_receive.at[step, way],
            device_id={"gx": me_x + move_x, "gy": me_y + move_y},
            device_id_type=MESH,
        )

    def band_copy(number, step, way):
        move_x, move_y = COMPASS[way]
        band = bands[number].at[step]
        from_x, to_x = strip(move_x, band.shape[0] - 2)
        from_y, to_y = strip(move_y, band.shape[1] - 2)
        if move_x != 0:
            from_y = to_y = pl.ds(0, band.shape[1])
        return pltpu.make_async_remote_copy(
            src_ref=band.at[from_x, from_y],
            dst_ref=band.at[to_x, to_y],
            send_sem=band_send.at[number, step, way],
            recv_sem=band_receive.at[number, step, way],
            device_id={"gx": me_x + move_x, "gy": me_y + move_y},
            device_id_type=MESH,
        )

    def near_copies(step):
        return [functools.partial(near_copy, step)]

    def band_copies(step):
        return [functools.partial(band_copy, number, step) for number in range(inner)]

    along_x = [(COMPASS.index((move, 0)), move, 0) for move in (-1, 1)]
    along_y = [(COMPASS.index((0, move)), 0, move) for move in (-1, 1)]
    corners = [(COMPASS.index((a, b)), a, 0) for a in (-1, 1) for b in (-1, 1)]

    def start_copies(copies, ways):
        for way, move_x, move_y in ways:

            @pl.when(inside(me_x + move_x, me_y + move_y))
            def _(way=way):
                for copy in copies:
                    copy(way).start()

    def finish_copies(copies, ways):
        for way, move_x, move_y in ways:

            @pl.when(inside(me_x + move_x, me_y + move_y))
            def _(way=way):
                for copy in copies:
                    copy(way).wait_send()

            @pl.when(inside(me_x - move_x, me_y - move_y))
            def _(way=way):
                for copy in copies:
                    copy(way).wait_recv()

    def cut_edges(step):
        for i, y in enumerate((0, side - 1)):
            for part in range(width // 128):
                line = product_of[part, pl.ds(y, side * fields, stride=side), :]
                edge_send[step, i, :, part * 128 : (part + 1) * 128] = line.astype(BF16)

    def upward(step):
        own = source[step, 1, slab : slab + rows]
        skeleton[0:rows, 0:rank] = product(own, basis[...], 0)
        parents = []
        for x in range(0, side, 2):
            for y in range(0, side, 2):
                four = [
                    skeleton[pl.ds((x + c) * slab + y + e, 8, stride=side), :][:, :rank]
                    for c, e in CHILDREN
                ]
                parents.append(jnp.concatenate(four, axis=1))
        span = side
        for depth in range(inner):
            span //= 2
            for i, parent in enumerate(parents):
                bands[depth][step, 1 + i // span, 1 + i % span] = parent
            level = times(jnp.concatenate(parents, axis=0), lift_high[depth], lift_low[depth])
            if depth < inner - 1:
                parents = group(level, span, span)
        mine[step] = level
        gathered[step, me] = level

    def gather_of(step):
        return mine.at[step], gathered.at[step], gather_send.at[step], gather_receive.at[step]

    table = near_lookup()

    def near_term(step, a, b, columns):
        piece = source[step, 1 + b, (1 + a) * slab : (1 + a) * slab + rows]
        return near_product(a, b, piece, columns)

    def near_product(a, b, piece, columns):
        slot, flipped = table[(a, b)]
        if flipped:
            return product(piece, near[slot, columns, :], 0)
        return product(piece, near[slot, :, columns])

    pieces = chunk // 128
    row_of = lax.broadcasted_iota(jnp.int32, (side, chunk), 0)

    def shift_rows(step, b, x, own, columns):
        shifted = []
        for field in range(fields):
            value = own[field * side : (field + 1) * side]
            value = pltpu.roll(value, side - 1 if b > 0 else 1, 0)
            shifted.append(jnp.where(row_of == (side - 1 if b > 0 else 0), 0.0, value))
        for field in range(0, fields, 2):
            begin = (x + 1) * slab + field * side
            source[step, 1 + b, begin : begin + 2 * side, columns] = jnp.concatenate(
                shifted[field : field + 2], axis=0
            ).astype(BF16)

    def over_columns(work):
        def one(index, carry):
            work(index, pl.ds(pl.multiple_of(index * chunk, chunk), chunk))
            return carry

        lax.fori_loop(0, width // chunk, one, 0)

    def couple(depth, window):
        value = None
        for i, (a, b) in enumerate(HALF_RING):
            for sign in (1, -1):
                term = times(
                    window(sign * a, sign * b),
                    far[depth, i, 0],
                    far[depth, i, 1],
                    1 if sign > 0 else 0,
                )
                value = term if value is None else value + term
        return value

    def near_local(step):
        def straight(index, columns):
            put(total, index * pieces, slice(0, rows), near_term(step, 0, 0, columns))
            for x in range(side):
                own = get(product_of, index * pieces, slice(x * slab, (x + 1) * slab), pieces)
                shift_rows(step, -1, x, own, columns)
                shift_rows(step, 1, x, own, columns)

        over_columns(straight)

        def level(index, columns):
            value = get(total, index * pieces, slice(0, rows), pieces)
            for b in (-1, 1):
                value = value + near_term(step, 0, b, columns)
            put(total, index * pieces, slice(0, rows), value)

        over_columns(level)

    def beyond_edges(step):
        finish_copies(near_copies(step), corners)
        last = fields * (side + 1)
        for i, b in enumerate((1, -1)):
            low, high = COMPASS.index((1, -b)), COMPASS.index((-1, -b))
            beyond[i, 0:fields] = corner[step, low].astype(F32)[16 - fields :]
            beyond[i, fields:last] = edge[step, i].astype(F32)
            beyond[i, last : last + fields] = corner[step, high].astype(F32)[:fields]

        def one(index, columns):
            for i, b in enumerate((1, -1)):
                value = None
                for a in (-1, 0, 1):
                    begin = (1 + a) * fields
                    piece = beyond[i, begin : begin + fields * side].astype(BF16)
                    term = near_product(a, b, piece, columns)
                    value = term if value is None else value + term
                place = pl.ds(side - 1 if b > 0 else 0, fields * side, stride=side)
                old = get(total, index * pieces, place, pieces)
                put(total, index * pieces, place, old + value)

        over_columns(one)

    def near_and_far(step):
        finish_copies(near_copies(step), along_x)
        for x in (-1, side):
            for begin in range(0, width, chunk):
                columns = slice(begin, begin + chunk)
                own = source[step, 1, (x + 1) * slab : (x + 2) * slab, columns].astype(F32)
                shift_rows(step, -1, x, own, columns)
                shift_rows(step, 1, x, own, columns)

        def sideways(index, columns):
            value = get(total, index * pieces, slice(0, rows), pieces)
            for a in (-1, 1):
                for b in (-1, 0, 1):
                    value = value + near_term(step, a, b, columns)
            put(total, index * pieces, slice(0, rows), value)

        over_columns(sideways)
        finish_copies(band_copies(step), along_y)
        start_copies(band_copies(step), along_x)
        finish_gather(*gather_of(step))
        across, along = size_x, size_y
        boxes = gathered[step].reshape(devices * 8, rank)
        for up in range(coarse):
            parents = group(boxes, across, along)
            across, along = across // 2, along // 2
            for i, parent in enumerate(parents):
                tops[up][1 + i // along, 1 + i % along] = parent
            if up < coarse - 1:
                boxes = times(
                    jnp.concatenate(parents, axis=0), lift_high[inner + up], lift_low[inner + up]
                )
        down = None
        for up in range(coarse - 1, -1, -1):
            near_x, near_y = me_x >> up + 1, me_y >> up + 1
            value = couple(
                inner + up, lambda a, b: tops[up][near_x + (1 + a), near_y + (1 + b)]
            )
            if down is not None:
                value = value + times(down, lift_high[inner + up], lift_low[inner + up], 0)
            child = 2 * (me_x >> up & 1) + (me_y >> up & 1)
            down = jnp.zeros((8, rank), F32)
            for i in range(4):
                down = jnp.where(child == i, value[:, i * rank : (i + 1) * rank], down)
        finish_copies(near_copies(step), along_y)
        start_copies(near_copies(step), corners)
        finish_copies(band_copies(step), along_x)
        here = []
        span = side
        for depth in range(inner):
            span //= 2
            here.append(
                couple(
                    depth,
                    lambda a, b: bands[depth][
                        step, 1 + a : 1 + a + span, 1 + b : 1 + b + span
                    ].reshape(span * span * 8, 4 * rank),
                )
            )
        span = 1
        for depth in range(inner - 1, -1, -1):
            value = here[depth] + times(down, lift_high[depth], lift_low[depth], 0)
            if depth > 0:
                down = ungroup(value, span, span)
            span *= 2
        for x in range(side):
            for y in range(side):
                place = pl.ds(x * slab + y, fields, stride=side)
                box = child_of(value, x, y, side // 2)
                skeleton[place, :] = jnp.concatenate([box, box], axis=1)[:fields]
        down = skeleton[0:rows, 0:rank]
        high = down.astype(BF16).astype(F32)
        both = jnp.concatenate([high, down - high], axis=1).astype(BF16)
        beyond_edges(step)
        for begin in range(0, width, 256):
            value = product(both, basis_twice[:, begin : begin + 256])
            amount = value.shape[1] // 128
            everywhere = slice(0, rows)
            put(total, begin // 128, everywhere, get(total, begin // 128, everywhere, amount) + value)

    for i in (0, 1, 2):
        loads[i].wait()
    skeleton[rows:, :] = jnp.zeros((skeleton.shape[0] - rows, skeleton.shape[1]), F32)
    diagonal = lax.broadcasted_iota(jnp.int32, (side, side), 0) == lax.broadcasted_iota(
        jnp.int32, (side, side), 1
    )

    def begin_first(x, add):
        line = jnp.broadcast_to(occupied[pl.ds(x, 1), :].astype(F32), (side, side))
        column = jnp.sum(jnp.where(diagonal, line, 0.0), axis=1, keepdims=True)
        wide = column * contrast[x]
        weight[x] = wide
        values = {}
        for field, part, place in tiles(x):
            value = rhs[x, field, part]
            add(0, field, value * value)
            values[field, part] = wide * value
            put(product_of, part * splits, place, values[field, part])
        put_source(0, x, values)

    put_sums(0, sweep(1, begin_first))
    cut_edges(0)
    loads[4].wait()
    loads[5].wait()
    for depth in range(levels - 1):
        lift_high[depth], lift_low[depth] = halves(lifts[depth])
    basis_twice[0:rank] = basis[...]
    basis_twice[rank:] = basis[...]
    upward(0)

    loads[3].wait()
    near_local(0)

    pl.semaphore_wait(barrier, devices - 1)
    start_copies(near_copies(0), along_x)
    start_copies(band_copies(0), along_y)
    start_gather(*gather_of(0))
    start_copies(near_copies(0), along_y)
    start_gather(*sums_of(0))
    loads[6].wait()

    def build(depth, carry):
        far_level(depth, coupling, far)
        return carry

    lax.fori_loop(0, levels, build, 0)
    near_and_far(0)

    (square_rhs,) = finish_sums(0, 1)
    beta = jnp.sqrt(square_rhs + EPSILON)
    inverse = 1.0 / beta
    norm_first = square_rhs / (square_rhs + EPSILON)

    by_beta = spread(inverse)

    def begin_second(x, add):
        wide = weight[x] * SHRINK
        values = {}
        for field, part, place in tiles(x):
            value = get(total, part * splits, place, splits) * by_beta[field]
            put(image, part * splits, place, value)
            add(0, field, rhs[x, field, part] * by_beta[field] * value)
            add(1, field, value * value)
            values[field, part] = wide * value
            put(product_of, part * splits, place, values[field, part])
        put_source(1, x, values)

    sums = sweep(2, begin_second)
    cut_edges(1)
    start_copies(near_copies(1), along_x)
    image_copy = pltpu.make_async_copy(image, image_out, unload.at[0])
    image_copy.start()
    upward(1)
    start_copies(band_copies(1), along_y)
    start_gather(*gather_of(1))
    start_copies(near_copies(1), along_y)
    put_sums(1, sums)
    start_gather(*sums_of(1))
    near_local(1)
    near_and_far(1)
    total_copy = pltpu.make_async_copy(total, total_out, unload.at[1])
    total_copy.start()

    along, square = finish_sums(1, 2)
    h11 = norm_first + along
    excess = h11 - 1.0
    square = square - 2.0 * excess * along + excess * excess * norm_first
    h21 = jnp.sqrt(square + EPSILON)
    inverse_second = 1.0 / h21
    norm_second = square / (square + EPSILON)
    cross = (along - excess * norm_first) * inverse_second
    grow, back = inverse_second * (1.0 / SHRINK), -excess * inverse_second

    of_second, by_excess, by_grow = spread(inverse_second), spread(excess), spread(grow)
    by_back = spread(back)

    def second_sums(x, add):
        for field, part, place in tiles(x):
            first = rhs[x, field, part] * by_beta[field]
            held = get(image, part * splits, place, splits)
            second = (held - by_excess[field] * first) * of_second[field]
            value = get(total, part * splits, place, splits) * by_grow[field]
            value = value + held * by_back[field]
            add(0, field, first * value)
            add(1, field, second * value)
            add(2, field, value * value)

    put_sums(2, sweep(3, second_sums))
    start_gather(*sums_of(2))
    on_first, on_second, square = finish_sums(2, 3)
    h12 = cross + on_first
    h22 = norm_second + on_second
    over = h22 - 1.0
    square = (
        square
        + h12 * h12 * norm_first
        + over * over * norm_second
        - 2.0 * h12 * on_first
        - 2.0 * over * on_second
        + 2.0 * h12 * over * cross
    )
    h32 = jnp.sqrt(square + EPSILON)
    inverse_third = 1.0 / h32
    columns = [beta, h11, h21, h12, h22, h32]
    columns.append(grow * inverse_third)
    columns.append((back - over * inverse_second) * inverse_third)
    columns.append((over * excess * inverse_second - h12) * inverse_third * inverse)
    tile = jnp.zeros((8, 128), F32)
    for i, column in enumerate(columns):
        tile = jnp.where(lane == i, column, tile)
    numbers[...] = tile
    image_copy.wait()
    total_copy.wait()


def combine_kernel(rhs_far, image_far, total_far, numbers, third_far, hess, *scratch):
    rhs, image, total, third, load, unload = scratch
    side, fields, comps, _, voxels = rhs.shape
    splits = voxels // 128
    slab = fields * side

    def copies(x):
        lines = pl.ds(x * slab, slab)
        return [
            pltpu.make_async_copy(rhs_far.at[x], rhs.at[x], load.at[0, x]),
            pltpu.make_async_copy(image_far.at[:, lines], image.at[:, lines], load.at[1, x]),
            pltpu.make_async_copy(total_far.at[:, lines], total.at[:, lines], load.at[2, x]),
        ]

    def result(x):
        return pltpu.make_async_copy(third.at[x], third_far.at[x], unload.at[x])

    for x in range(side):
        for copy in copies(x):
            copy.start()
    hess[...] = numbers[:fields, :6]
    by = [
        [jnp.broadcast_to(numbers[field : field + 1, i : i + 1], (side, 128)) for i in (6, 7, 8)]
        for field in range(fields)
    ]
    for x in range(side):
        for copy in copies(x):
            copy.wait()
        for field in range(fields):
            of_total, of_image, of_rhs = by[field]
            place = slice((x * fields + field) * side, (x * fields + field + 1) * side)
            for part in range(comps):
                for i in range(splits):
                    at = part * splits + i
                    lanes = slice(i * 128, (i + 1) * 128)
                    third[x, field, part, :, lanes] = (
                        total[at, place] * of_total
                        + image[at, place] * of_image
                        + rhs[x, field, part, :, lanes] * of_rhs
                    )
        result(x).start()
    for x in range(side):
        result(x).wait()


def combine(rhs, image, total, numbers):
    side, fields = rhs.shape[:2]
    anywhere = pl.BlockSpec(memory_space=pl.ANY)
    here = pl.BlockSpec(memory_space=pltpu.VMEM)
    return pl.pallas_call(
        combine_kernel,
        in_specs=[anywhere, anywhere, anywhere, here],
        out_specs=[anywhere, here],
        out_shape=[
            jax.ShapeDtypeStruct(rhs.shape, F32),
            jax.ShapeDtypeStruct((fields, 6), F32),
        ],
        scratch_shapes=[
            pltpu.VMEM(rhs.shape, F32),
            pltpu.VMEM(image.shape, F32),
            pltpu.VMEM(total.shape, F32),
            pltpu.VMEM(rhs.shape, F32),
            pltpu.SemaphoreType.DMA((3, side)),
            pltpu.SemaphoreType.DMA((side,)),
        ],
    )(rhs, image, total, numbers)


def krylov(rhs, contrast, occupied, near, basis, lifts, coupling, count, size_x, size_y):
    side, fields, comps, _, voxels = rhs.shape
    rank, width = basis.shape
    inner = side.bit_length() - 1
    levels = coupling.shape[0]
    coarse = levels - inner
    devices = size_x * size_y
    slab = fields * side
    rows = side * slab
    ways = len(COMPASS)
    arguments = (rhs, contrast, occupied, near, basis, lifts, coupling)
    scratch = [pltpu.VMEM(value.shape, value.dtype) for value in arguments]
    scratch += [
        pltpu.VMEM((levels, len(HALF_RING), 2, 4 * rank, 4 * rank), BF16),
        pltpu.VMEM((levels - 1, 4 * rank, rank), BF16),
        pltpu.VMEM((levels - 1, 4 * rank, rank), BF16),
        pltpu.VMEM((2 * rank, width), BF16),
        pltpu.VMEM(contrast.shape, F32),
        pltpu.VMEM((width // 128, rows, 128), F32),
        pltpu.VMEM((2, 3, rows + 2 * slab, width), BF16),
        pltpu.VMEM((width // 128, rows, 128), F32),
        pltpu.VMEM((width // 128, rows, 128), F32),
        pltpu.VMEM((rows + 2 * side, 128), F32),
        pltpu.VMEM((2, 2, side * fields, width), BF16),
        pltpu.VMEM((2, 2, side * fields, width), BF16),
        pltpu.VMEM((2, ways, 16, width), BF16),
        pltpu.VMEM((2, (side + 3) * fields, width), F32),
    ]
    for depth in range(inner):
        span = (side >> depth + 1) + 2
        scratch.append(pltpu.VMEM((2, span, span, 8, 4 * rank), F32))
    for up in range(coarse):
        grid = ((size_x >> up + 1) + 2, (size_y >> up + 1) + 2)
        scratch.append(pltpu.VMEM(grid + (8, 4 * rank), F32))
    scratch += [
        pltpu.VMEM((2, 8, rank), F32),
        pltpu.VMEM((2, devices, 8, rank), F32),
        pltpu.VMEM((3, 1, 128), F32),
        pltpu.VMEM((3, devices, 1, 128), F32),
        pltpu.SemaphoreType.DMA((2, ways)),
        pltpu.SemaphoreType.DMA((2, ways)),
        pltpu.SemaphoreType.DMA((inner, 2, ways)),
        pltpu.SemaphoreType.DMA((inner, 2, ways)),
        pltpu.SemaphoreType.DMA((2,)),
        pltpu.SemaphoreType.DMA((2,)),
        pltpu.SemaphoreType.DMA((3,)),
        pltpu.SemaphoreType.DMA((3,)),
        pltpu.SemaphoreType.DMA((len(arguments),)),
        pltpu.SemaphoreType.DMA((2,)),
    ]
    anywhere = pl.BlockSpec(memory_space=pl.ANY)
    return pl.pallas_call(
        functools.partial(krylov_kernel, size_x, size_y, inner, count),
        in_specs=[anywhere] * len(arguments),
        out_specs=[anywhere, anywhere, pl.BlockSpec(memory_space=pltpu.VMEM)],
        out_shape=[
            jax.ShapeDtypeStruct((width // 128, rows, 128), F32),
            jax.ShapeDtypeStruct((width // 128, rows, 128), F32),
            jax.ShapeDtypeStruct((8, 128), F32),
        ],
        scratch_shapes=scratch,
        compiler_params=pltpu.CompilerParams(collective_id=0, has_side_effects=True),
    )(*arguments)


def body(rhs, contrast, occupied, near, basis, transfer, coupling):
    side, _, _, parts, voxels = rhs.shape
    rank = basis.shape[1]
    devices_x = lax.axis_size("gx")
    devices_y = lax.axis_size("gy")
    count = float(side * side * devices_x * devices_y * parts * voxels)
    lifts = transfer.reshape(transfer.shape[0], 4 * rank, rank)
    flat = rhs.transpose(0, 2, 3, 1, 4)
    image, total, numbers = krylov(
        flat,
        contrast,
        occupied,
        near,
        basis.T,
        lifts,
        coupling,
        count,
        devices_x,
        devices_y,
    )
    third, hess = combine(flat, image, total, numbers)
    return (third.transpose(0, 3, 1, 2, 4), hess)


def solution(mesh):
    placed = (
        P("gx", "gy", None, None, None),
        P("gx", "gy", None),
        P("gx", "gy"),
        P(),
        P(),
        P(),
        P(),
    )
    return jax.shard_map(
        body,
        mesh=mesh,
        in_specs=placed,
        out_specs=(P("gx", "gy", None, None, None), P()),
        check_vma=False,
    )
```

```python
import functools

import jax
import jax.numpy as jnp
from jax import lax
from jax.experimental import pallas as pl
from jax.experimental.pallas import tpu as pltpu
from jax.sharding import PartitionSpec as P

EPSILON = 1e-06
SHRINK = 2.0**-20
NEAR_BASE = ((0, 0), (1, -1), (1, 0), (1, 1), (0, 1))
HALF_RING = NEAR_BASE[1:]
AROUND = [(a, b) for a in (-1, 0, 1) for b in (-1, 0, 1)]
COMPASS = [d for d in AROUND if d != (0, 0)]
CHILDREN = [(c, e) for c in (0, 1) for e in (0, 1)]
MESH = pl.DeviceIdType.MESH
F32 = jnp.float32
BF16 = jnp.bfloat16


def near_lookup():
    table = {}
    for slot, (a, b) in enumerate(NEAR_BASE):
        table[(a, b)] = (slot, False)
        if (a, b) != (0, 0):
            table[(-a, -b)] = (slot, True)
    return table


def far_lookup():
    base = [
        (a, b)
        for a in range(-3, 4)
        for b in range(-3, 4)
        if max(abs(a), abs(b)) >= 2 and (a > 0 or (a == 0 and b > 0))
    ]
    table = {}
    for slot, (a, b) in enumerate(base):
        table[(a, b)] = (slot, False)
        table[(-a, -b)] = (slot, True)
    return table


def halves(values):
    high = values.astype(BF16)
    return high, (values - high.astype(F32)).astype(BF16)


def far_level(depth, coupling, far):
    table = far_lookup()
    rank = coupling.shape[2]
    empty = jnp.zeros((rank, rank), F32)
    seen = {}

    def block_of(offset):
        if offset not in table:
            return empty
        if offset not in seen:
            slot, flipped = table[offset]
            block = coupling[depth, slot]
            seen[offset] = block.T if flipped else block
        return seen[offset]

    for i, (px, py) in enumerate(HALF_RING):
        for k, (c, e) in enumerate(CHILDREN):
            line = [block_of((2 * px + c - tc, 2 * py + e - te)) for tc, te in CHILDREN]
            high, low = halves(jnp.concatenate(line, axis=1))
            far[depth, i, 0, k * rank : (k + 1) * rank, :] = high
            far[depth, i, 1, k * rank : (k + 1) * rank, :] = low


def strip(move, length):
    if move > 0:
        return pl.ds(length, 1), pl.ds(0, 1)
    if move < 0:
        return pl.ds(1, 1), pl.ds(length + 1, 1)
    return pl.ds(1, length), pl.ds(1, length)


def stacked(values):
    high = values.astype(BF16).astype(F32)
    return jnp.concatenate([high, values - high], axis=0).astype(BF16)


def product(left, right, across=1):
    return lax.dot_general(
        left, right, (((1,), (1 - across,)), ((), ())), preferred_element_type=F32
    )


def times(values, high, low, across=1):
    both = stacked(values)
    total = product(both, high, across) + product(both, low, across)
    rows = values.shape[0]
    return total[:rows] + total[rows:]


def group(boxes, size_x, size_y):
    rows = []
    for x in range(0, size_x, 2):
        for y in range(0, size_y, 2):
            four = [(x + c) * size_y + y + e for c, e in CHILDREN]
            rows.append(jnp.concatenate([boxes[8 * i : 8 * i + 8] for i in four], axis=1))
    return rows


def child_of(parents, x, y, size_y):
    rank = parents.shape[1] // 4
    i = (x // 2) * size_y + y // 2
    k = 2 * (x % 2) + y % 2
    return parents[8 * i : 8 * i + 8, k * rank : (k + 1) * rank]


def ungroup(parents, size_x, size_y):
    return jnp.concatenate(
        [child_of(parents, x, y, size_y) for x in range(2 * size_x) for y in range(2 * size_y)],
        axis=0,
    )


def clear_rim(out):
    long_x, long_y = out.shape[0], out.shape[1]
    line_x = jnp.zeros((1,) + out.shape[1:], out.dtype)
    line_y = jnp.zeros((long_x, 1) + out.shape[2:], out.dtype)
    out[0:1] = line_x
    out[long_x - 1 : long_x] = line_x
    out[:, 0:1] = line_y
    out[:, long_y - 1 : long_y] = line_y


def fold(value):
    pieces = [value[:, i : i + 128] for i in range(0, value.shape[1], 128)]
    return functools.reduce(lambda a, b: a + b, pieces)


def krylov_kernel(size_x, size_y, inner, count, *refs):
    arguments, (image_out, total_out, numbers), scratch = refs[:7], refs[7:10], refs[10:]
    rhs, contrast, occupied, near, basis, lifts, coupling = scratch[:7]
    far, lift_high, lift_low, basis_twice, weight, product_of, source = scratch[7:14]
    image, total, skeleton, edge_send, edge, corner, beyond = scratch[14:21]
    bands = scratch[21 : 21 + inner]
    rest = scratch[21 + inner :]
    levels = coupling.shape[0]
    coarse = levels - inner
    tops = rest[:coarse]
    mine, gathered, parts, slots = rest[coarse : coarse + 4]
    near_send, near_receive, band_send, band_receive = rest[coarse + 4 : coarse + 8]
    gather_send, gather_receive, sum_send, sum_receive, load, unload = rest[coarse + 8 :]

    side, fields, comps, _, voxels = rhs.shape
    rank, width = basis.shape
    slab = fields * side
    rows = side * slab
    devices = size_x * size_y
    me_x, me_y = lax.axis_index("gx"), lax.axis_index("gy")
    me = me_x * size_y + me_y
    chunk = 256 if width % 256 == 0 else 128
    lane = lax.broadcasted_iota(jnp.int32, (8, 128), 1)
    sublane = lax.broadcasted_iota(jnp.int32, (8, 128), 0)

    loads = [
        pltpu.make_async_copy(argument, here, load.at[i])
        for i, (argument, here) in enumerate(zip(arguments, scratch[:7]))
    ]
    for i in (0, 1, 2, 4, 5, 6, 3):
        loads[i].start()

    def wrap(value, size):
        return jnp.where(value >= size, value - size, value)

    def others(act):
        def line(shift_x):
            to_x, from_x = wrap(me_x + shift_x, size_x), wrap(me_x + size_x - shift_x, size_x)
            for shift_y in range(size_y):
                if not isinstance(shift_x, int) or (shift_x, shift_y) != (0, 0):
                    to_y = wrap(me_y + shift_y, size_y)
                    from_y = wrap(me_y + size_y - shift_y, size_y)
                    act(shift_x * size_y + shift_y, (to_x, to_y), from_x * size_y + from_y)

        if devices <= 64:
            for shift_x in range(size_x):
                line(shift_x)
        else:
            line(0)

            def one(shift_x, carry):
                line(shift_x)
                return carry

            lax.fori_loop(1, size_x, one, 0)

    for step in (0, 1):
        for side_rows in (slice(0, slab), slice((side + 1) * slab, (side + 2) * slab)):
            source[step, 1, side_rows] = jnp.zeros((slab, width), BF16)
        edge[step] = jnp.zeros(edge.shape[1:], BF16)
        corner[step] = jnp.zeros(corner.shape[1:], BF16)
        for band in bands:
            clear_rim(band.at[step])
    for top in tops:
        clear_rim(top)

    barrier = pltpu.get_barrier_semaphore()

    def greet(step, to, before):
        pl.semaphore_signal(
            barrier, inc=1, device_id={"gx": to[0], "gy": to[1]}, device_id_type=MESH
        )

    others(greet)

    def gather_copy(piece, target, sent, received, to, slot):
        return pltpu.make_async_remote_copy(
            src_ref=piece,
            dst_ref=target.at[slot],
            send_sem=sent,
            recv_sem=received,
            device_id={"gx": to[0], "gy": to[1]},
            device_id_type=MESH,
        )

    def start_gather(*what):
        others(lambda step, to, before: gather_copy(*what, to, me).start())

    def finish_gather(piece, target, sent, received):
        bulk = target.at[pl.ds(0, devices - 1)]
        pltpu.make_async_copy(bulk, bulk, received).wait()
        pltpu.make_async_copy(bulk, bulk, sent).wait()

    def sums_of(number):
        return parts.at[number], slots.at[number], sum_send.at[number], sum_receive.at[number]

    def put_sums(number, sums):
        tile = jnp.zeros((8, 128), F32)
        for i, of_fields in enumerate(sums):
            lines = [jnp.sum(value, axis=0, keepdims=True) for value in of_fields]
            lines.append(jnp.zeros((8 - fields, 128), F32))
            column = jnp.sum(jnp.concatenate(lines, axis=0), axis=1, keepdims=True)
            tile = tile + jnp.where(lane == 8 * i + sublane, column, 0.0)
        line = jnp.sum(tile, axis=0, keepdims=True)
        parts[number] = line
        slots[number, me] = line

    def finish_sums(number, amount):
        finish_gather(*sums_of(number))
        line = jnp.broadcast_to(jnp.sum(slots[number], axis=0) * (1.0 / count), (8, 128))
        return [
            jnp.sum(jnp.where(lane == 8 * i + sublane, line, 0.0), axis=1, keepdims=True)
            for i in range(amount)
        ]

    def spread(column):
        return [
            jnp.broadcast_to(column[field : field + 1, :], (8, voxels)) for field in range(fields)
        ]

    def sweep(amount, work):
        zero = tuple(jnp.zeros((8, 128), F32) for _ in range(amount * fields))

        def one(x, sums):
            sums = [list(sums[i * fields : (i + 1) * fields]) for i in range(amount)]

            def add(i, field, value):
                sums[i][field] = sums[i][field] + fold(value)

            work(x, add)
            return tuple(value for of_fields in sums for value in of_fields)

        out = lax.fori_loop(0, side, one, zero)
        return [out[i * fields : (i + 1) * fields] for i in range(amount)]

    def tiles(x):
        for field in range(fields):
            place = pl.ds(pl.multiple_of(x * slab + field * side, 8), side)
            for part in range(comps):
                yield field, part, place

    def put(target, begin, place, value):
        for i in range(value.shape[1] // 128):
            target[begin + i, place] = value[:, i * 128 : (i + 1) * 128]

    def get(target, begin, place, amount):
        return jnp.concatenate([target[begin + i, place] for i in range(amount)], axis=1)

    splits = voxels // 128

    def put_source(step, x, values):
        for field in range(0, fields, 2):
            place = pl.ds(pl.multiple_of((x + 1) * slab + field * side, 16), 2 * side)
            for part in range(comps):
                pair = [values[field + i, part] for i in (0, 1)]
                columns = slice(part * voxels, (part + 1) * voxels)
                source[step, 1, place, columns] = jnp.concatenate(pair, axis=0).astype(BF16)

    def inside(place_x, place_y):
        return (place_x >= 0) & (place_x < size_x) & (place_y >= 0) & (place_y < size_y)

    def near_copy(step, way):
        move_x, move_y = COMPASS[way]
        if move_y == 0:
            begin, end = (side, 0) if move_x > 0 else (1, side + 1)
            from_ref = source.at[step, 1, pl.ds(begin * slab, slab)]
            to_ref = source.at[step, 1, pl.ds(end * slab, slab)]
        else:
            from_ref = edge_send.at[step, int(move_y > 0)]
            to_ref = edge.at[step, int(move_y > 0)]
            if move_x != 0:
                begin = from_ref.shape[0] - 16 if move_x > 0 else 0
                from_ref, to_ref = to_ref.at[pl.ds(begin, 16)], corner.at[step, way]
                move_y = 0
        return pltpu.make_async_remote_copy(
            src_ref=from_ref,
            dst_ref=to_ref,
            send_sem=near_send.at[step, way],
            recv_sem=near_receive.at[step, way],
            device_id={"gx": me_x + move_x, "gy": me_y + move_y},
            device_id_type=MESH,
        )

    def band_copy(number, step, way):
        move_x, move_y = COMPASS[way]
        band = bands[number].at[step]
        from_x, to_x = strip(move_x, band.shape[0] - 2)
        from_y, to_y = strip(move_y, band.shape[1] - 2)
        if move_x != 0:
            from_y = to_y = pl.ds(0, band.shape[1])
        return pltpu.make_async_remote_copy(
            src_ref=band.at[from_x, from_y],
            dst_ref=band.at[to_x, to_y],
            send_sem=band_send.at[number, step, way],
            recv_sem=band_receive.at[number, step, way],
            device_id={"gx": me_x + move_x, "gy": me_y + move_y},
            device_id_type=MESH,
        )

    def near_copies(step):
        return [functools.partial(near_copy, step)]

    def band_copies(step):
        return [functools.partial(band_copy, number, step) for number in range(inner)]

    along_x = [(COMPASS.index((move, 0)), move, 0) for move in (-1, 1)]
    along_y = [(COMPASS.index((0, move)), 0, move) for move in (-1, 1)]
    corners = [(COMPASS.index((a, b)), a, 0) for a in (-1, 1) for b in (-1, 1)]

    def start_copies(copies, ways):
        for way, move_x, move_y in ways:

            @pl.when(inside(me_x + move_x, me_y + move_y))
            def _(way=way):
                for copy in copies:
                    copy(way).start()

    def finish_copies(copies, ways):
        for way, move_x, move_y in ways:

            @pl.when(inside(me_x + move_x, me_y + move_y))
            def _(way=way):
                for copy in copies:
                    copy(way).wait_send()

            @pl.when(inside(me_x - move_x, me_y - move_y))
            def _(way=way):
                for copy in copies:
                    copy(way).wait_recv()

    def cut_edges(step):
        for i, y in enumerate((0, side - 1)):
            for part in range(width // 128):
                line = product_of[part, pl.ds(y, side * fields, stride=side), :]
                edge_send[step, i, :, part * 128 : (part + 1) * 128] = line.astype(BF16)

    def upward(step):
        own = source[step, 1, slab : slab + rows]
        skeleton[0:rows, 0:rank] = product(own, basis[...], 0)
        parents = []
        for x in range(0, side, 2):
            for y in range(0, side, 2):
                four = [
                    skeleton[pl.ds((x + c) * slab + y + e, 8, stride=side), :][:, :rank]
                    for c, e in CHILDREN
                ]
                parents.append(jnp.concatenate(four, axis=1))
        span = side
        for depth in range(inner):
            span //= 2
            for i, parent in enumerate(parents):
                bands[depth][step, 1 + i // span, 1 + i % span] = parent
            level = times(jnp.concatenate(parents, axis=0), lift_high[depth], lift_low[depth])
            if depth < inner - 1:
                parents = group(level, span, span)
        mine[step] = level
        gathered[step, me] = level

    def gather_of(step):
        return mine.at[step], gathered.at[step], gather_send.at[step], gather_receive.at[step]

    table = near_lookup()

    def near_term(step, a, b, columns):
        piece = source[step, 1 + b, (1 + a) * slab : (1 + a) * slab + rows]
        return near_product(a, b, piece, columns)

    def near_product(a, b, piece, columns):
        slot, flipped = table[(a, b)]
        if flipped:
            return product(piece, near[slot, columns, :], 0)
        return product(piece, near[slot, :, columns])

    pieces = chunk // 128
    row_of = lax.broadcasted_iota(jnp.int32, (side, chunk), 0)

    def shift_rows(step, b, x, own, columns):
        shifted = []
        for field in range(fields):
            value = own[field * side : (field + 1) * side]
            value = pltpu.roll(value, side - 1 if b > 0 else 1, 0)
            shifted.append(jnp.where(row_of == (side - 1 if b > 0 else 0), 0.0, value))
        for field in range(0, fields, 2):
            begin = (x + 1) * slab + field * side
            source[step, 1 + b, begin : begin + 2 * side, columns] = jnp.concatenate(
                shifted[field : field + 2], axis=0
            ).astype(BF16)

    def over_columns(work):
        def one(index, carry):
            work(index, pl.ds(pl.multiple_of(index * chunk, chunk), chunk))
            return carry

        lax.fori_loop(0, width // chunk, one, 0)

    def couple(depth, window):
        value = None
        for i, (a, b) in enumerate(HALF_RING):
            for sign in (1, -1):
                term = times(
                    window(sign * a, sign * b),
                    far[depth, i, 0],
                    far[depth, i, 1],
                    1 if sign > 0 else 0,
                )
                value = term if value is None else value + term
        return value

    def near_local(step):
        def straight(index, columns):
            put(total, index * pieces, slice(0, rows), near_term(step, 0, 0, columns))
            for x in range(side):
                own = get(product_of, index * pieces, slice(x * slab, (x + 1) * slab), pieces)
                shift_rows(step, -1, x, own, columns)
                shift_rows(step, 1, x, own, columns)

        over_columns(straight)

        def level(index, columns):
            value = get(total, index * pieces, slice(0, rows), pieces)
            for b in (-1, 1):
                value = value + near_term(step, 0, b, columns)
            put(total, index * pieces, slice(0, rows), value)

        over_columns(level)

    def beyond_edges(step):
        finish_copies(near_copies(step), corners)
        last = fields * (side + 1)
        for i, b in enumerate((1, -1)):
            low, high = COMPASS.index((1, -b)), COMPASS.index((-1, -b))
            beyond[i, 0:fields] = corner[step, low].astype(F32)[16 - fields :]
            beyond[i, fields:last] = edge[step, i].astype(F32)
            beyond[i, last : last + fields] = corner[step, high].astype(F32)[:fields]

        def one(index, columns):
            for i, b in enumerate((1, -1)):
                value = None
                for a in (-1, 0, 1):
                    begin = (1 + a) * fields
                    piece = beyond[i, begin : begin + fields * side].astype(BF16)
                    term = near_product(a, b, piece, columns)
                    value = term if value is None else value + term
                place = pl.ds(side - 1 if b > 0 else 0, fields * side, stride=side)
                old = get(total, index * pieces, place, pieces)
                put(total, index * pieces, place, old + value)

        over_columns(one)

    def near_and_far(step):
        finish_copies(near_copies(step), along_x)
        for x in (-1, side):
            for begin in range(0, width, chunk):
                columns = slice(begin, begin + chunk)
                own = source[step, 1, (x + 1) * slab : (x + 2) * slab, columns].astype(F32)
                shift_rows(step, -1, x, own, columns)
                shift_rows(step, 1, x, own, columns)

        def sideways(index, columns):
            value = get(total, index * pieces, slice(0, rows), pieces)
            for a in (-1, 1):
                for b in (-1, 0, 1):
                    value = value + near_term(step, a, b, columns)
            put(total, index * pieces, slice(0, rows), value)

        over_columns(sideways)
        finish_copies(band_copies(step), along_y)
        start_copies(band_copies(step), along_x)
        finish_gather(*gather_of(step))
        across, along = size_x, size_y
        boxes = gathered[step].reshape(devices * 8, rank)
        for up in range(coarse):
            parents = group(boxes, across, along)
            across, along = across // 2, along // 2
            for i, parent in enumerate(parents):
                tops[up][1 + i // along, 1 + i % along] = parent
            if up < coarse - 1:
                boxes = times(
                    jnp.concatenate(parents, axis=0), lift_high[inner + up], lift_low[inner + up]
                )
        down = None
        for up in range(coarse - 1, -1, -1):
            near_x, near_y = me_x >> up + 1, me_y >> up + 1
            value = couple(
                inner + up, lambda a, b: tops[up][near_x + (1 + a), near_y + (1 + b)]
            )
            if down is not None:
                value = value + times(down, lift_high[inner + up], lift_low[inner + up], 0)
            child = 2 * (me_x >> up & 1) + (me_y >> up & 1)
            down = jnp.zeros((8, rank), F32)
            for i in range(4):
                down = jnp.where(child == i, value[:, i * rank : (i + 1) * rank], down)
        finish_copies(near_copies(step), along_y)
        start_copies(near_copies(step), corners)
        finish_copies(band_copies(step), along_x)
        here = []
        span = side
        for depth in range(inner):
            span //= 2
            here.append(
                couple(
                    depth,
                    lambda a, b: bands[depth][
                        step, 1 + a : 1 + a + span, 1 + b : 1 + b + span
                    ].reshape(span * span * 8, 4 * rank),
                )
            )
        span = 1
        for depth in range(inner - 1, -1, -1):
            value = here[depth] + times(down, lift_high[depth], lift_low[depth], 0)
            if depth > 0:
                down = ungroup(value, span, span)
            span *= 2
        for x in range(side):
            for y in range(side):
                place = pl.ds(x * slab + y, fields, stride=side)
                box = child_of(value, x, y, side // 2)
                skeleton[place, :] = jnp.concatenate([box, box], axis=1)[:fields]
        down = skeleton[0:rows, 0:rank]
        high = down.astype(BF16).astype(F32)
        both = jnp.concatenate([high, down - high], axis=1).astype(BF16)
        beyond_edges(step)
        for begin in range(0, width, 256):
            value = product(both, basis_twice[:, begin : begin + 256])
            amount = value.shape[1] // 128
            everywhere = slice(0, rows)
            put(total, begin // 128, everywhere, get(total, begin // 128, everywhere, amount) + value)

    for i in (0, 1, 2):
        loads[i].wait()
    skeleton[rows:, :] = jnp.zeros((skeleton.shape[0] - rows, skeleton.shape[1]), F32)
    diagonal = lax.broadcasted_iota(jnp.int32, (side, side), 0) == lax.broadcasted_iota(
        jnp.int32, (side, side), 1
    )

    def begin_first(x, add):
        line = jnp.broadcast_to(occupied[pl.ds(x, 1), :].astype(F32), (side, side))
        column = jnp.sum(jnp.where(diagonal, line, 0.0), axis=1, keepdims=True)
        wide = column * contrast[x]
        weight[x] = wide
        values = {}
        for field, part, place in tiles(x):
            value = rhs[x, field, part]
            add(0, field, value * value)
            values[field, part] = wide * value
            put(product_of, part * splits, place, values[field, part])
        put_source(0, x, values)

    put_sums(0, sweep(1, begin_first))
    cut_edges(0)
    loads[4].wait()
    loads[5].wait()
    for depth in range(levels - 1):
        lift_high[depth], lift_low[depth] = halves(lifts[depth])
    basis_twice[0:rank] = basis[...]
    basis_twice[rank:] = basis[...]
    upward(0)

    loads[6].wait()

    def build(depth, carry):
        far_level(depth, coupling, far)
        return carry

    lax.fori_loop(0, levels, build, 0)

    pl.semaphore_wait(barrier, devices - 1)
    start_copies(near_copies(0), along_x)
    start_copies(band_copies(0), along_y)
    start_gather(*gather_of(0))
    start_copies(near_copies(0), along_y)
    start_gather(*sums_of(0))
    loads[3].wait()
    near_local(0)

    near_and_far(0)

    (square_rhs,) = finish_sums(0, 1)
    beta = jnp.sqrt(square_rhs + EPSILON)
    inverse = 1.0 / beta
    norm_first = square_rhs / (square_rhs + EPSILON)

    by_beta = spread(inverse)

    def begin_second(x, add):
        wide = weight[x] * SHRINK
        values = {}
        for field, part, place in tiles(x):
            value = get(total, part * splits, place, splits) * by_beta[field]
            put(image, part * splits, place, value)
            add(0, field, rhs[x, field, part] * by_beta[field] * value)
            add(1, field, value * value)
            values[field, part] = wide * value
            put(product_of, part * splits, place, values[field, part])
        put_source(1, x, values)

    sums = sweep(2, begin_second)
    cut_edges(1)
    start_copies(near_copies(1), along_x)
    image_copy = pltpu.make_async_copy(image, image_out, unload.at[0])
    image_copy.start()
    upward(1)
    start_copies(band_copies(1), along_y)
    start_gather(*gather_of(1))
    start_copies(near_copies(1), along_y)
    put_sums(1, sums)
    start_gather(*sums_of(1))
    near_local(1)
    near_and_far(1)
    total_copy = pltpu.make_async_copy(total, total_out, unload.at[1])
    total_copy.start()

    along, square = finish_sums(1, 2)
    h11 = norm_first + along
    excess = h11 - 1.0
    square = square - 2.0 * excess * along + excess * excess * norm_first
    h21 = jnp.sqrt(square + EPSILON)
    inverse_second = 1.0 / h21
    norm_second = square / (square + EPSILON)
    cross = (along - excess * norm_first) * inverse_second
    grow, back = inverse_second * (1.0 / SHRINK), -excess * inverse_second

    of_second, by_excess, by_grow = spread(inverse_second), spread(excess), spread(grow)
    by_back = spread(back)

    def second_sums(x, add):
        for field, part, place in tiles(x):
            first = rhs[x, field, part] * by_beta[field]
            held = get(image, part * splits, place, splits)
            second = (held - by_excess[field] * first) * of_second[field]
            value = get(total, part * splits, place, splits) * by_grow[field]
            value = value + held * by_back[field]
            add(0, field, first * value)
            add(1, field, second * value)
            add(2, field, value * value)

    put_sums(2, sweep(3, second_sums))
    start_gather(*sums_of(2))
    on_first, on_second, square = finish_sums(2, 3)
    h12 = cross + on_first
    h22 = norm_second + on_second
    over = h22 - 1.0
    square = (
        square
        + h12 * h12 * norm_first
        + over * over * norm_second
        - 2.0 * h12 * on_first
        - 2.0 * over * on_second
        + 2.0 * h12 * over * cross
    )
    h32 = jnp.sqrt(square + EPSILON)
    inverse_third = 1.0 / h32
    columns = [beta, h11, h21, h12, h22, h32]
    columns.append(grow * inverse_third)
    columns.append((back - over * inverse_second) * inverse_third)
    columns.append((over * excess * inverse_second - h12) * inverse_third * inverse)
    tile = jnp.zeros((8, 128), F32)
    for i, column in enumerate(columns):
        tile = jnp.where(lane == i, column, tile)
    numbers[...] = tile
    image_copy.wait()
    total_copy.wait()


def combine_kernel(rhs_far, image_far, total_far, numbers_far, third_far, hess_far, *scratch):
    rhs, image, total, numbers, third, hess, load, unload, small = scratch
    side, fields, comps, _, voxels = rhs.shape
    splits = voxels // 128
    slab = fields * side

    def copies(x):
        lines = pl.ds(x * slab, slab)
        return [
            pltpu.make_async_copy(rhs_far.at[x], rhs.at[x], load.at[0, x]),
            pltpu.make_async_copy(image_far.at[:, lines], image.at[:, lines], load.at[1, x]),
            pltpu.make_async_copy(total_far.at[:, lines], total.at[:, lines], load.at[2, x]),
        ]

    def result(x):
        return pltpu.make_async_copy(third.at[x], third_far.at[x], unload.at[x])

    numbers_copy = pltpu.make_async_copy(numbers_far, numbers, small.at[0])
    hess_copy = pltpu.make_async_copy(hess, hess_far, small.at[1])
    numbers_copy.start()
    for x in range(side):
        for copy in copies(x):
            copy.start()
    numbers_copy.wait()
    hess[...] = numbers[:fields, :6]
    hess_copy.start()
    by = [
        [jnp.broadcast_to(numbers[field : field + 1, i : i + 1], (side, 128)) for i in (6, 7, 8)]
        for field in range(fields)
    ]
    for x in range(side):
        for copy in copies(x):
            copy.wait()
        for field in range(fields):
            of_total, of_image, of_rhs = by[field]
            place = slice((x * fields + field) * side, (x * fields + field + 1) * side)
            for part in range(comps):
                for i in range(splits):
                    at = part * splits + i
                    lanes = slice(i * 128, (i + 1) * 128)
                    third[x, field, part, :, lanes] = (
                        total[at, place] * of_total
                        + image[at, place] * of_image
                        + rhs[x, field, part, :, lanes] * of_rhs
                    )
        result(x).start()
    for x in range(side):
        result(x).wait()
    hess_copy.wait()


def combine(rhs, image, total, numbers):
    side, fields = rhs.shape[:2]
    anywhere = pl.BlockSpec(memory_space=pl.ANY)
    return pl.pallas_call(
        combine_kernel,
        in_specs=[anywhere] * 4,
        out_specs=[anywhere] * 2,
        out_shape=[
            jax.ShapeDtypeStruct(rhs.shape, F32),
            jax.ShapeDtypeStruct((fields, 6), F32),
        ],
        scratch_shapes=[
            pltpu.VMEM(rhs.shape, F32),
            pltpu.VMEM(image.shape, F32),
            pltpu.VMEM(total.shape, F32),
            pltpu.VMEM(numbers.shape, F32),
            pltpu.VMEM(rhs.shape, F32),
            pltpu.VMEM((fields, 6), F32),
            pltpu.SemaphoreType.DMA((3, side)),
            pltpu.SemaphoreType.DMA((side,)),
            pltpu.SemaphoreType.DMA((2,)),
        ],
    )(rhs, image, total, numbers)


def krylov(rhs, contrast, occupied, near, basis, lifts, coupling, count, size_x, size_y):
    side, fields, comps, _, voxels = rhs.shape
    rank, width = basis.shape
    inner = side.bit_length() - 1
    levels = coupling.shape[0]
    coarse = levels - inner
    devices = size_x * size_y
    slab = fields * side
    rows = side * slab
    ways = len(COMPASS)
    arguments = (rhs, contrast, occupied, near, basis, lifts, coupling)
    scratch = [pltpu.VMEM(value.shape, value.dtype) for value in arguments]
    scratch += [
        pltpu.VMEM((levels, len(HALF_RING), 2, 4 * rank, 4 * rank), BF16),
        pltpu.VMEM((levels - 1, 4 * rank, rank), BF16),
        pltpu.VMEM((levels - 1, 4 * rank, rank), BF16),
        pltpu.VMEM((2 * rank, width), BF16),
        pltpu.VMEM(contrast.shape, F32),
        pltpu.VMEM((width // 128, rows, 128), F32),
        pltpu.VMEM((2, 3, rows + 2 * slab, width), BF16),
        pltpu.VMEM((width // 128, rows, 128), F32),
        pltpu.VMEM((width // 128, rows, 128), F32),
        pltpu.VMEM((rows + 2 * side, 128), F32),
        pltpu.VMEM((2, 2, side * fields, width), BF16),
        pltpu.VMEM((2, 2, side * fields, width), BF16),
        pltpu.VMEM((2, ways, 16, width), BF16),
        pltpu.VMEM((2, (side + 3) * fields, width), F32),
    ]
    for depth in range(inner):
        span = (side >> depth + 1) + 2
        scratch.append(pltpu.VMEM((2, span, span, 8, 4 * rank), F32))
    for up in range(coarse):
        grid = ((size_x >> up + 1) + 2, (size_y >> up + 1) + 2)
        scratch.append(pltpu.VMEM(grid + (8, 4 * rank), F32))
    scratch += [
        pltpu.VMEM((2, 8, rank), F32),
        pltpu.VMEM((2, devices, 8, rank), F32),
        pltpu.VMEM((3, 1, 128), F32),
        pltpu.VMEM((3, devices, 1, 128), F32),
        pltpu.SemaphoreType.DMA((2, ways)),
        pltpu.SemaphoreType.DMA((2, ways)),
        pltpu.SemaphoreType.DMA((inner, 2, ways)),
        pltpu.SemaphoreType.DMA((inner, 2, ways)),
        pltpu.SemaphoreType.DMA((2,)),
        pltpu.SemaphoreType.DMA((2,)),
        pltpu.SemaphoreType.DMA((3,)),
        pltpu.SemaphoreType.DMA((3,)),
        pltpu.SemaphoreType.DMA((len(arguments),)),
        pltpu.SemaphoreType.DMA((2,)),
    ]
    anywhere = pl.BlockSpec(memory_space=pl.ANY)
    return pl.pallas_call(
        functools.partial(krylov_kernel, size_x, size_y, inner, count),
        in_specs=[anywhere] * len(arguments),
        out_specs=[anywhere, anywhere, pl.BlockSpec(memory_space=pltpu.VMEM)],
        out_shape=[
            jax.ShapeDtypeStruct((width // 128, rows, 128), F32),
            jax.ShapeDtypeStruct((width // 128, rows, 128), F32),
            jax.ShapeDtypeStruct((8, 128), F32),
        ],
        scratch_shapes=scratch,
        compiler_params=pltpu.CompilerParams(collective_id=0, has_side_effects=True),
    )(*arguments)


def body(rhs, contrast, occupied, near, basis, transfer, coupling):
    side, _, _, parts, voxels = rhs.shape
    rank = basis.shape[1]
    devices_x = lax.axis_size("gx")
    devices_y = lax.axis_size("gy")
    count = float(side * side * devices_x * devices_y * parts * voxels)
    lifts = transfer.reshape(transfer.shape[0], 4 * rank, rank)
    flat = rhs.transpose(0, 2, 3, 1, 4)
    image, total, numbers = krylov(
        flat,
        contrast,
        occupied,
        near,
        basis.T,
        lifts,
        coupling,
        count,
        devices_x,
        devices_y,
    )
    third, hess = combine(flat, image, total, numbers)
    return (third.transpose(0, 3, 1, 2, 4), hess)


def solution(mesh):
    placed = (
        P("gx", "gy", None, None, None),
        P("gx", "gy", None),
        P("gx", "gy"),
        P(),
        P(),
        P(),
        P(),
    )
    return jax.shard_map(
        body,
        mesh=mesh,
        in_specs=placed,
        out_specs=(P("gx", "gy", None, None, None), P()),
        check_vma=False,
    )
```
